32 devices in a mesh: brick: 16 (over z, x, core), view: 2 (over y).
Axes of the slice: x: 2, y: 2, z: 4, core: 2. Of those that a mesh axis runs over, the one named last changes fastest.
Arguments:
- estimate: float32 [128, 64, 512], P('brick'), may hold values from 0.5 to 2
- camera_blocks: bfloat16 [2, 256, 8, 2048], P('view', 'brick'), may hold values from 0.099609375 to 2
- block_lists: int32 [2, 16, 16, 2], P('view'), may hold values from -1 to 15, as said below
- block_offsets: int32 [2, 256], P('view'), may hold values from 1 to 124, as said below
- psf_index: int32 [2, 64], P('view'), may hold values from 0 to 15
- psf_bank: float32 [2, 2, 16, 9], P('view'), may hold values from 0.03 to 0.3
Outputs:
- updated: float32 [128, 64, 512], P('brick')
The draws below stay inside these ranges and needn't reach their ends.
Inputs may be any that keep to these rules, and one draw needn't show every extreme that they name: block_lists[v, d, s] names exactly the blocks of holder s that intersect brick d, each once; at most 2 of them, and 2 for some brick and holder. `block_offsets`: every block starts after its brick's first row by 1 to 4 rows.
All inputs are finite; a program needn't handle non-finite values.
Results may differ from the reference program's by a relative error of at most 0.0003.
Values may be sent and summed in bfloat16 or wider, within the bound.
No kernel may reach another device: no remote copies, remote signals or barrier semaphores. Data moves between devices by JAX's collectives and lax.ppermute only.
A program may use at most 128 MiB of HBM per device.

```python
import math
import jax
import jax.numpy as jnp
from jax import lax

VIEWS = 2
X_DEV = 8
NX = 128
NZ = 64
NY = 512
TY = 32
TILES_DEV = 16
CAP = 2
NKERN = 16
TAPS = 9


def layout_tables(key):
    brick_count = NX // X_DEV
    radius = TAPS // 2

    def one_view(view_key):
        key_first, key_rest, key_jit = jax.random.split(view_key, 3)
        first_shift = jax.random.randint(key_first, (), 0, brick_count).astype(jnp.int32)
        others = jax.random.permutation(key_rest, brick_count - 2)[:TILES_DEV - 2].astype(jnp.int32)
        shifts = jnp.concatenate([jnp.stack([first_shift, (first_shift + 1) % brick_count]), (first_shift + 2 + others) % brick_count]).astype(jnp.int32)
        jitter = jax.random.randint(key_jit, (brick_count, TILES_DEV), 1, radius + 1).astype(jnp.int32)
        low_source = (brick_count - shifts[0]) % brick_count
        high_source = (brick_count - 1 - shifts[0]) % brick_count
        jitter = jitter.at[high_source, 0].set(radius).at[low_source, 0].set(1)
        source_ids = jnp.arange(brick_count, dtype=jnp.int32)
        x_rows = (source_ids[:, None] + shifts[None, :]) % brick_count
        offsets = (x_rows * X_DEV + jitter).reshape(-1)
        dest_ids = source_ids[:, None, None]
        block_ids = jnp.arange(TILES_DEV, dtype=jnp.int32)[None, None, :]
        same_row = x_rows[None, :, :] == dest_ids
        row_before = x_rows[None, :, :] == dest_ids - 1
        own_block = jnp.where(jnp.any(same_row, axis=2), jnp.sum(jnp.where(same_row, block_ids, 0), axis=2), -1)
        before = jnp.where(jnp.any(row_before, axis=2), jnp.sum(jnp.where(row_before, block_ids, 0), axis=2), -1)
        tables = jnp.stack([own_block, before], axis=-1)
        return (tables.astype(jnp.int32), offsets.astype(jnp.int32))
    return jax.vmap(one_view)(jax.random.split(key, VIEWS))


def draw_block_lists(key, part):
    return layout_tables(jax.random.fold_in(key, 17))[0]


def draw_block_offsets(key, part):
    return layout_tables(jax.random.fold_in(key, 17))[1]


def plant(values, key, smallest, top_value):
    longest = values.shape.index(max(values.shape))
    spots = []
    for shift in (0, 1):
        where = [jax.random.randint(jax.random.fold_in(key, axis), (), 0, length) for axis, length in enumerate(values.shape)]
        where[longest] = (where[longest] + shift) % values.shape[longest]
        spots.append(tuple(where))
    return values.at[spots[0]].set(smallest).at[spots[1]].set(top_value)


def shard_levels(stream_key, shape, cuts, smallest, high):
    level = 1.0
    for dim, parts in cuts:
        heights = jax.random.uniform(jax.random.fold_in(jax.random.fold_in(stream_key, 6), dim), (parts,), jnp.float32, smallest / len(cuts), high / len(cuts))
        level = level * jnp.repeat(jnp.exp(heights), shape[dim] // parts).reshape((-1,) + (1,) * (len(shape) - 1 - dim))
    return level


def setup_inputs(seed: int = 0) -> dict:
    streams_of = jax.random.split(jax.random.key(seed), 7)
    estimate = jnp.clip(0.5 + 1.5 * jax.random.uniform(streams_of[0], (NX, NZ, NY), jnp.float32) ** shard_levels(streams_of[0], (NX, NZ, NY), ((0, 16),), -0.2, 0.2), 0.5, 2.0)
    camera_blocks = jnp.clip(jnp.exp(math.log(2.0) - 2.9996462 * jax.random.uniform(streams_of[1], (VIEWS, NX // X_DEV * TILES_DEV, X_DEV, NZ * TY), jnp.float32) ** shard_levels(streams_of[1], (VIEWS, NX // X_DEV * TILES_DEV, X_DEV, NZ * TY), ((0, 2), (1, 16)), -0.2, 0.2)), 0.099609375, 2.0).astype(jnp.bfloat16)
    block_lists = draw_block_lists(jax.random.fold_in(streams_of[6], 71), 0)
    block_offsets = draw_block_offsets(jax.random.fold_in(streams_of[6], 71), 0)
    psf_index = plant(jax.random.randint(streams_of[4], (VIEWS, NZ), 0, NKERN), jax.random.fold_in(streams_of[4], 1), 0, NKERN - 1).astype(jnp.int32)
    psf_bank = jnp.clip(jnp.exp(math.log(0.3) - 2.3025852 * jax.random.uniform(streams_of[5], (VIEWS, 2, NKERN, TAPS), jnp.float32) ** shard_levels(streams_of[5], (VIEWS, 2, NKERN, TAPS), ((0, 2),), -0.2, 0.2)), 0.03, 0.3)
    return {"estimate": estimate, "camera_blocks": camera_blocks, "block_lists": block_lists, "block_offsets": block_offsets, "psf_index": psf_index, "psf_bank": psf_bank}


def blur_cols(field, kern, reverse):
    tap_count = kern.shape[1]
    radius = tap_count // 2
    width = field.shape[2]
    padded = jnp.pad(field, ((0, 0), (0, 0), (radius, radius)))
    result = None
    for offset in range(tap_count):
        begin_at = 2 * radius - offset if reverse else offset
        term = kern[:, offset][None, :, None] * padded[:, :, begin_at:begin_at + width]
        result = term if result is None else result + term
    return result


def blur_rows(padded, kern, reverse, rows):
    tap_count = kern.shape[1]
    radius = tap_count // 2
    result = None
    for offset in range(tap_count):
        begin_at = 2 * radius - offset if reverse else offset
        term = kern[:, offset][None, :, None] * padded[begin_at:begin_at + rows]
        result = term if result is None else result + term
    return result


def assemble(blocks_view, lists_view, offsets_view):
    brick_count = NX // X_DEV
    canvas = jnp.zeros((NX + 2 * X_DEV, NZ, NY), jnp.float32)

    def place_one(index, canvas):
        index = jnp.asarray(index).astype(jnp.int32)
        dest_id = index // (brick_count * CAP)
        source_id = (index // CAP) % brick_count
        slot_id = index % CAP
        block_id = lists_view[dest_id, source_id, slot_id].astype(jnp.int32)
        is_valid = block_id >= 0
        safe_id = jnp.maximum(block_id, 0).astype(jnp.int32)
        global_id = (source_id * TILES_DEV + safe_id).astype(jnp.int32)
        block_data = lax.dynamic_index_in_dim(blocks_view, global_id, 0, keepdims=False)
        block_data = block_data.astype(jnp.float32).reshape(X_DEV, NZ, TY)
        row_start = offsets_view[global_id].astype(jnp.int32)
        row_ids = row_start + jnp.arange(X_DEV).astype(jnp.int32)
        row_keep = (row_ids >= dest_id * X_DEV) & (row_ids < (dest_id + 1) * X_DEV) & is_valid
        block_data = block_data * row_keep[:, None, None].astype(jnp.float32)
        corner = ((row_start + X_DEV).astype(jnp.int32), jnp.zeros((), jnp.int32), (safe_id * TY).astype(jnp.int32))
        previous = lax.dynamic_slice(canvas, corner, block_data.shape)
        return lax.dynamic_update_slice(canvas, previous + block_data, corner)

    canvas = lax.fori_loop(0, brick_count * brick_count * CAP, place_one, canvas)
    return canvas[X_DEV:X_DEV + NX]


def reference(estimate, camera_blocks, block_lists, block_offsets, psf_index, psf_bank):
    radius = TAPS // 2
    product = None
    for view_id in range(VIEWS):
        kern_x = psf_bank[view_id, 0][psf_index[view_id]]
        kern_y = psf_bank[view_id, 1][psf_index[view_id]]
        measured = assemble(camera_blocks[view_id], block_lists[view_id], block_offsets[view_id])
        padded = jnp.pad(estimate, ((radius, radius), (0, 0), (0, 0)))
        blurred = blur_rows(blur_cols(padded, kern_y, False), kern_x, False, NX)
        ratio = measured / blurred
        padded_ratio = jnp.pad(ratio, ((radius, radius), (0, 0), (0, 0)))
        correction = blur_rows(blur_cols(padded_ratio, kern_y, True), kern_x, True, NX)
        product = correction if product is None else product * correction
    return estimate * product
```

```python
import functools

import jax
import jax.numpy as jnp
from jax import lax
from jax.experimental import pallas as pl
from jax.experimental.pallas import tpu as pltpu
from jax.sharding import PartitionSpec as P

LANES = 128
SUBLANES = 8
VMEM = pl.BlockSpec(memory_space=pltpu.VMEM)
SMEM = pl.BlockSpec(memory_space=pltpu.SMEM)


def tile(ref, row, group, col):
    return ref[row, pl.ds(group * SUBLANES, SUBLANES), pl.ds(col * LANES, LANES)]


def shifted(tiles, lane, shift):
    if shift == 0:
        return tiles
    zero = jnp.zeros_like(tiles[0])
    rolled = [pltpu.roll(t, (-shift) % LANES, 1) for t in tiles]
    if shift > 0:
        ahead = rolled[1:] + [zero]
        return [jnp.where(lane < LANES - shift, a, b) for a, b in zip(rolled, ahead)]
    behind = [zero] + rolled[:-1]
    return [jnp.where(lane >= -shift, a, b) for a, b in zip(rolled, behind)]


def blur_row(source, row, group, wx, wy, taps, reverse, lane, cols):
    radius = taps // 2
    planes = pl.ds(group * SUBLANES, SUBLANES)
    sums = None
    for tap in range(taps):
        at = row + (2 * radius - tap if reverse else tap)
        weight = wx[tap, planes, :]
        terms = [weight * tile(source, at, group, col) for col in range(cols)]
        sums = terms if sums is None else [a + b for a, b in zip(sums, terms)]
    result = None
    for tap in range(taps):
        weight = wy[tap, planes, :]
        moved = shifted(sums, lane, radius - tap if reverse else tap - radius)
        terms = [weight * m for m in moved]
        result = terms if result is None else [a + b for a, b in zip(result, terms)]
    return result


def pack_body(spot, lists, blocks, out):
    chips, cores, views, slots, _, width = out.shape
    bricks = chips * cores
    here = spot[0]

    def one_chip(chip, carry):
        for slot in range(slots):
            at = ((cores * chip + cores - 1) * bricks + here) * slots + slot
            block = jnp.maximum(lists[at], 0)
            for core in range(cores):
                for view in range(views):
                    begin = (view * cores + core) * width
                    out[chip, core, view, slot] = blocks[block, :, begin : begin + width]
        return carry

    lax.fori_loop(0, chips, one_chip, 0)


def blur_body(layout, spot, table, top, low, high, bottom, blurred, wx, wy, field):
    views, part, cores, taps, kernels = (
        layout["views"], layout["part"], layout["cores"], layout["taps"], layout["kernels"])
    where = spot[1] * cores + spot[2]
    for view in range(views):
        base = view * layout["table"]

        def one_plane(plane, carry):
            pick = table[base + layout["index_at"] + where * part + plane].astype(jnp.int32)
            for axis, target in enumerate((wx, wy)):
                begin = base + layout["bank_at"] + (axis * kernels + pick) * taps
                for tap in range(taps):
                    target[tap, pl.ds(view * part + plane, 1), :] = jnp.full(
                        (1, LANES), table[begin + tap], jnp.float32)
            return carry

        lax.fori_loop(0, part, one_plane, 0)
        planes = slice(view * part, (view + 1) * part)
        at = 0
        for piece in (top, low, high, bottom):
            rows = piece.shape[0]
            field[at : at + rows, planes, :] = piece[...]
            at += rows
    rows_out, planes, columns = blurred.shape
    lane = lax.broadcasted_iota(jnp.int32, (SUBLANES, LANES), 1)

    def one_row(row, carry):
        for group in range(planes // SUBLANES):
            tiles = blur_row(field, row, group, wx, wy, taps, False, lane, columns // LANES)
            for col, value in enumerate(tiles):
                blurred[row, pl.ds(group * SUBLANES, SUBLANES), pl.ds(col * LANES, LANES)] = value
        return carry

    lax.fori_loop(0, rows_out, one_row, 0)


def ratio_body(layout, spot, table, arrived, blurred, ratio, placed, turned):
    views, cores, slots = layout["views"], layout["cores"], layout["slots"]
    bricks, per_holder, rows_dev = layout["bricks"], layout["per_holder"], layout["rows_dev"]
    rows_out, planes, columns = ratio.shape
    per_tile = LANES // layout["block_width"]
    depth_tiles = layout["part"] // per_tile
    groups = views * depth_tiles
    pitch = layout["pitch"]
    chip = lax.div(spot[0], cores)
    first_row = chip * cores * rows_dev
    placed[...] = jnp.zeros_like(placed)

    def one_source(source, carry):
        adds = []
        for view in range(views):
            base = view * layout["table"]
            for slot in range(slots):
                at = ((cores * chip + cores - 1) * bricks + source) * slots + slot
                listed = table[base + at].astype(jnp.int32)
                named = listed >= 0
                block = jnp.maximum(listed, 0)
                start = table[base + layout["offset_at"] + source * per_holder + block]
                start = jnp.where(named, start.astype(jnp.int32) - first_row, 0)
                target = jnp.where(named, block, per_holder)
                values = arrived[source * views + view, slot].astype(jnp.float32)
                for z_tile in range(depth_tiles):
                    begin = (target * groups + view * depth_tiles + z_tile) * pitch + start
                    adds.append((begin, values[:, z_tile * LANES : (z_tile + 1) * LANES]))
        held = [placed[pl.ds(begin, rows_dev), :] for begin, _ in adds]
        for (begin, value), old in zip(adds, held):
            placed[pl.ds(begin, rows_dev), :] = old + value
        return carry

    lax.fori_loop(0, bricks, one_source, 0)

    lane = lax.broadcasted_iota(jnp.int32, (groups, LANES), 1)
    own_rows = cores * rows_dev
    keep_spill = (chip < bricks // cores - 1).astype(jnp.float32)

    def one_row(row, carry):
        for col in range(columns // LANES):
            tiles = [
                placed[pl.ds((col * per_tile + k) * groups * pitch + row, groups, stride=pitch), :]
                for k in range(per_tile)
            ]
            step = per_tile // 2
            while step:
                width = step * layout["block_width"]
                first_half = (lane // width) % 2 == 0
                mixed = list(tiles)
                for k in range(per_tile):
                    if (k // step) % 2 == 0:
                        a, b = tiles[k], tiles[k + step]
                        mixed[k] = jnp.where(first_half, a, pltpu.roll(b, width, 1))
                        mixed[k + step] = jnp.where(first_half, pltpu.roll(a, LANES - width, 1), b)
                tiles = mixed
                step //= 2
            for k, value in enumerate(tiles):
                turned[pl.ds(col * planes + k, groups, stride=per_tile), :] = value
        scale = jnp.where(row < own_rows, 1.0, keep_spill)
        for col in range(columns // LANES):
            for group in range(planes // SUBLANES):
                measured = turned[pl.ds(col * planes + group * SUBLANES, SUBLANES), :]
                ratio[row, pl.ds(group * SUBLANES, SUBLANES), pl.ds(col * LANES, LANES)] = (
                    measured * scale / tile(blurred, row, group, col))
        return carry

    lax.fori_loop(0, rows_out, one_row, 0)


def correct_body(layout, spot, ratio, before, after, wx, wy, low, high, keep, send, field, done):
    views, part, cores, taps = layout["views"], layout["part"], layout["cores"], layout["taps"]
    rows_all, planes, columns = ratio.shape
    spill = after.shape[0]
    own_rows = rows_all - spill
    rows_dev = own_rows // cores
    field[0:spill] = before[0:spill]
    field[spill : 2 * spill] = ratio[0:spill] + before[spill : 2 * spill]
    field[2 * spill : spill + own_rows] = ratio[spill:own_rows]
    field[spill + own_rows :] = ratio[own_rows:] + after[...]
    lane = lax.broadcasted_iota(jnp.int32, (SUBLANES, LANES), 1)

    def one_row(row, carry):
        for group in range(planes // SUBLANES):
            tiles = blur_row(field, row, group, wx, wy, taps, True, lane, columns // LANES)
            for col, value in enumerate(tiles):
                done[row, pl.ds(group * SUBLANES, SUBLANES), pl.ds(col * LANES, LANES)] = value
        return carry

    lax.fori_loop(0, own_rows, one_row, 0)
    core = spot[2]

    def finish(half, source, target):
        rows = pl.ds(half * rows_dev, rows_dev)
        product = done[rows, 0:part, :]
        for view in range(1, views):
            product = product * done[rows, view * part : (view + 1) * part, :]
        target[...] = source * product

    mine = jnp.where(core == 0, low[...], high[...])
    theirs = jnp.where(core == 0, high[...], low[...])
    finish(core, mine, keep)
    finish(1 - core, theirs, send)


def join_body(spot, keep, near, far, far_near, out):
    view, core = spot[1], spot[2]
    part = keep.shape[1]
    for v, c, piece in (
        (view, core, keep), (view, 1 - core, near), (1 - view, core, far), (1 - view, 1 - core, far_near)):
        out[:, pl.ds(pl.multiple_of((v * 2 + c) * part, part), part), :] = piece[...]


def shards(estimate, camera_blocks, block_lists, block_offsets, psf_index, psf_bank):
    rows_dev, depth, columns = estimate.shape
    _, per_holder, block_rows, block_lanes = camera_blocks.shape
    bricks, slots = block_lists.shape[1], block_lists.shape[3]
    views = lax.axis_size("view")
    kernels, taps = psf_bank.shape[2:]
    radius = taps // 2
    cores = 2
    chips = bricks // cores
    part = depth // (cores * views)
    planes = views * part
    block_width = block_lanes // depth
    brick = lax.axis_index("brick")
    view = lax.axis_index("view")
    core = lax.rem(brick, cores)
    spot = jnp.stack([brick, view, core]).astype(jnp.int32)
    f32 = jnp.float32

    lists = block_lists[0].reshape(-1)
    packed = pl.pallas_call(
        pack_body,
        out_shape=jax.ShapeDtypeStruct(
            (chips, cores, views, slots, block_rows, part * block_width), camera_blocks.dtype),
        in_specs=[SMEM, SMEM, VMEM],
        out_specs=VMEM,
        name="pack",
    )(spot, lists, camera_blocks[0])
    packed = packed.reshape(bricks * views, slots, block_rows, part * block_width)
    arrived = lax.all_to_all(packed, ("brick", "view"), 0, 0, tiled=True)

    pieces = [lists, block_offsets[0], psf_index[0], psf_bank[0].reshape(-1)]
    starts = [0]
    for piece in pieces:
        starts.append(starts[-1] + piece.shape[0])
    length = -(-starts[-1] // LANES) * LANES
    table = jnp.concatenate(
        [piece.astype(f32) for piece in pieces] + [jnp.zeros((length - starts[-1],), f32)])
    if views == 2:
        other = lax.ppermute(table, "view", [(0, 1), (1, 0)])
        table = jnp.concatenate(
            [jnp.where(view == 0, table, other), jnp.where(view == 0, other, table)])
    else:
        table = lax.all_gather(table, "view", tiled=True)
    layout = dict(
        views=views, part=part, cores=cores, taps=taps, kernels=kernels, slots=slots, bricks=bricks,
        per_holder=per_holder, rows_dev=rows_dev, block_width=block_width, table=length,
        offset_at=starts[1], index_at=starts[2], bank_at=starts[3],
        pitch=cores * rows_dev + 2 * radius)

    parts = estimate.reshape(rows_dev, views, cores, part, columns)
    mine = parts[:, view, core]
    theirs = parts[:, view, 1 - core]
    swap = [(i, i ^ 1) for i in range(bricks)]
    up = [(i, i + cores) for i in range(bricks - cores)]
    down = [(i + cores, i) for i in range(bricks - cores)]
    partner = lax.ppermute(theirs, "brick", swap)
    low = jnp.where(core == 0, mine, partner)
    high = jnp.where(core == 0, partner, mine)
    top = lax.ppermute(high[rows_dev - radius :], "brick", up)
    bottom = lax.ppermute(low[: 2 * radius], "brick", down)

    own_rows = cores * rows_dev
    rows_all = own_rows + radius
    blurred, wx, wy = pl.pallas_call(
        functools.partial(blur_body, layout),
        out_shape=[
            jax.ShapeDtypeStruct((rows_all, planes, columns), f32),
            jax.ShapeDtypeStruct((taps, planes, LANES), f32),
            jax.ShapeDtypeStruct((taps, planes, LANES), f32),
        ],
        in_specs=[SMEM, SMEM] + [VMEM] * 4,
        out_specs=[VMEM] * 3,
        scratch_shapes=[pltpu.VMEM((rows_all + 2 * radius, planes, columns), f32)],
        name="blur",
    )(spot, table, top, low, high, bottom)

    groups = planes * block_width // LANES
    ratio = pl.pallas_call(
        functools.partial(ratio_body, layout),
        out_shape=jax.ShapeDtypeStruct((rows_all, planes, columns), f32),
        in_specs=[SMEM, SMEM, VMEM, VMEM],
        out_specs=VMEM,
        scratch_shapes=[
            pltpu.VMEM(((per_holder + 1) * groups * layout["pitch"], LANES), f32),
            pltpu.VMEM((columns // LANES * planes, LANES), f32),
        ],
        name="ratio",
    )(spot, table, arrived, blurred)

    before = lax.ppermute(ratio[own_rows - radius :], "brick", up)
    after = lax.ppermute(ratio[:radius], "brick", down)
    piece = jax.ShapeDtypeStruct((rows_dev, part, columns), f32)
    keep, send = pl.pallas_call(
        functools.partial(correct_body, layout),
        out_shape=[piece, piece],
        in_specs=[SMEM] + [VMEM] * 7,
        out_specs=[VMEM] * 2,
        scratch_shapes=[
            pltpu.VMEM((own_rows + 2 * radius, planes, columns), f32),
            pltpu.VMEM((own_rows, planes, columns), f32),
        ],
        name="correct",
    )(spot, ratio, before, after, wx, wy, low, high)

    if views == 2:
        turn = [(0, 1), (1, 0)]
        far = lax.ppermute(keep, "view", turn)
        near = lax.ppermute(send, "brick", swap)
        far_near = lax.ppermute(near, "view", turn)
        return pl.pallas_call(
            join_body,
            out_shape=jax.ShapeDtypeStruct(estimate.shape, f32),
            in_specs=[SMEM] + [VMEM] * 4,
            out_specs=VMEM,
            name="join",
        )(spot, keep, near, far, far_near)
    near = lax.ppermute(send, "brick", swap)
    both = jnp.stack([jnp.where(core == 0, keep, near), jnp.where(core == 0, near, keep)], axis=1)
    everything = lax.all_gather(both, "view")
    return everything.transpose(1, 0, 2, 3, 4).reshape(estimate.shape)


def solution(mesh):
    placed = (
        P("brick", None, None),
        P("view", "brick", None, None),
        P("view", None, None, None),
        P("view", None),
        P("view", None),
        P("view", None, None, None),
    )
    return jax.shard_map(
        shards, mesh=mesh, in_specs=placed, out_specs=P("brick", None, None), check_vma=False
    )
```

```python
import functools
import math

import jax
import jax.numpy as jnp
from jax import lax
from jax.experimental import pallas as pl
from jax.experimental.pallas import tpu as pltpu
from jax.sharding import PartitionSpec as P

CAMERA = (0.099609375, 2.0)
PSF = (0.03, 0.3)
ESTIMATE = (0.5, 2.0)
CODE_TOP = 32767.0
LANES = 128
SUBLANES = 8
GRANT = pltpu.CompilerParams(vmem_limit_bytes=12 << 20)
VMEM = pl.BlockSpec(memory_space=pltpu.VMEM)
HBM = pl.BlockSpec(memory_space=pl.ANY)
SMEM = pl.BlockSpec(memory_space=pltpu.SMEM)


def tile(ref, row, group, col):
    return ref[row, pl.ds(group * SUBLANES, SUBLANES), pl.ds(col * LANES, LANES)]


def shifted(tiles, lane, shift):
    if shift == 0:
        return tiles
    zero = jnp.zeros_like(tiles[0])
    rolled = [pltpu.roll(t, (-shift) % LANES, 1) for t in tiles]
    if shift > 0:
        ahead = rolled[1:] + [zero]
        return [jnp.where(lane < LANES - shift, a, b) for a, b in zip(rolled, ahead)]
    behind = [zero] + rolled[:-1]
    return [jnp.where(lane >= -shift, a, b) for a, b in zip(rolled, behind)]


def blur_row(source, row, group, wx, wy, taps, reverse, lane, cols):
    radius = taps // 2
    planes = pl.ds(group * SUBLANES, SUBLANES)
    sums = None
    for tap in range(taps):
        at = row + (2 * radius - tap if reverse else tap)
        weight = wx[tap, planes, :]
        terms = [weight * tile(source, at, group, col) for col in range(cols)]
        sums = terms if sums is None else [a + b for a, b in zip(sums, terms)]
    result = None
    for tap in range(taps):
        weight = wy[tap, planes, :]
        moved = shifted(sums, lane, radius - tap if reverse else tap - radius)
        terms = [weight * m for m in moved]
        result = terms if result is None else [a + b for a, b in zip(result, terms)]
    return result


def near_core(*values):
    return [pltpu.with_memory_space_constraint(value, pltpu.VMEM) for value in values]


def position(cores):
    brick = lax.axis_index("brick")
    return lax.div(brick, cores), lax.rem(brick, cores), lax.axis_index("view")


def ratio_range(bricks, taps):
    least = CAMERA[0] / (taps * taps * PSF[1] * PSF[1] * ESTIMATE[1])
    inside = taps // 2 + 1
    most = bricks * CAMERA[1] / (inside * inside * PSF[0] * PSF[0] * ESTIMATE[0])
    low, high = math.log(least) - 0.01, math.log(most) + 0.01
    return low, (high - low) / (2 * CODE_TOP - 1)


def encode_ratio(value, bricks, taps):
    low, step = ratio_range(bricks, taps)
    tiny = math.exp(low)
    code = jnp.round((jnp.log(jnp.maximum(value, tiny)) - low) * (1.0 / step)) + (1.0 - CODE_TOP)
    code = jnp.where(value > 0, jnp.minimum(code, CODE_TOP), -CODE_TOP)
    return code.astype(jnp.int32).astype(jnp.int16)


def decode_ratio(code, bricks, taps):
    low, step = ratio_range(bricks, taps)
    code = code.astype(jnp.int32).astype(jnp.float32)
    value = jnp.exp((code + (CODE_TOP - 1.0)) * step + low)
    return jnp.where(code > -CODE_TOP, value, 0.0)


def encode_estimate(value):
    scale = 2 * CODE_TOP / (ESTIMATE[1] - ESTIMATE[0])
    code = jnp.round((value - ESTIMATE[0]) * scale) - CODE_TOP
    return jnp.clip(code, -CODE_TOP, CODE_TOP).astype(jnp.int16)


def decode_estimate(code):
    scale = (ESTIMATE[1] - ESTIMATE[0]) / (2 * CODE_TOP)
    return (code.astype(jnp.int32).astype(jnp.float32) + CODE_TOP) * scale + ESTIMATE[0]


def pack_body(lists, blocks, out):
    chips, cores, views, slots, _, width = out.shape
    here = lax.axis_index("brick")

    def one_chip(chip, carry):
        for slot in range(slots):
            block = jnp.maximum(lists[cores * chip + cores - 1, slot, here], 0)
            for core in range(cores):
                for view in range(views):
                    begin = (view * cores + core) * width
                    out[chip, core, view, slot] = blocks[block, :, begin : begin + width]
        return carry

    lax.fori_loop(0, chips, one_chip, 0)


def blur_body(layout, table, top, low, high, bottom, inverse, wx, wy, field):
    views, part, cores, taps, kernels = (
        layout["views"], layout["part"], layout["cores"], layout["taps"], layout["kernels"])
    chip, core, view_here = position(cores)
    where = view_here * cores + core
    has_top = (chip > 0).astype(jnp.float32)
    has_bottom = (chip < layout["bricks"] // cores - 1).astype(jnp.float32)
    rows = (decode_estimate(top[...]) * has_top, low[...], high[...],
            decode_estimate(bottom[...]) * has_bottom)
    for view in range(views):
        base = view * layout["table"]

        def one_plane(plane, carry):
            pick = table[base + layout["index_at"] + where * part + plane].astype(jnp.int32)
            for axis, target in enumerate((wx, wy)):
                begin = base + layout["bank_at"] + (axis * kernels + pick) * taps
                for tap in range(taps):
                    target[tap, pl.ds(view * part + plane, 1), :] = jnp.full(
                        (1, LANES), table[begin + tap], jnp.float32)
            return carry

        lax.fori_loop(0, part, one_plane, 0)
        planes = slice(view * part, (view + 1) * part)
        at = 0
        for piece in rows:
            field[at : at + piece.shape[0], planes, :] = piece
            at += piece.shape[0]
    rows_out, planes, columns = inverse.shape
    own_rows = cores * layout["rows_dev"]
    lane = lax.broadcasted_iota(jnp.int32, (SUBLANES, LANES), 1)

    def one_row(row, carry):
        wanted = jnp.where(row < own_rows, 1.0, has_bottom)
        for group in range(planes // SUBLANES):
            tiles = blur_row(field, row, group, wx, wy, taps, False, lane, columns // LANES)
            for col, value in enumerate(tiles):
                inverse[row, pl.ds(group * SUBLANES, SUBLANES), pl.ds(col * LANES, LANES)] = wanted / value
        return carry

    lax.fori_loop(0, rows_out, one_row, 0, unroll=2)


def ratio_body(layout, table, arrived, inverse, field, upward, downward, placed, turned):
    views, cores, slots, taps = layout["views"], layout["cores"], layout["slots"], layout["taps"]
    bricks, per_holder, rows_dev = layout["bricks"], layout["per_holder"], layout["rows_dev"]
    rows_out, planes, columns = inverse.shape
    radius = taps // 2
    per_tile = LANES // layout["block_width"]
    depth_tiles = layout["part"] // per_tile
    groups = views * depth_tiles
    pitch = layout["pitch"]
    chip, _, _ = position(cores)
    first_row = chip * cores * rows_dev
    placed[...] = jnp.zeros_like(placed)

    def one_source(source, carry):
        adds = []
        for view in range(views):
            base = view * layout["table"]
            for slot in range(slots):
                listed = table[base + slot * bricks + source].astype(jnp.int32)
                named = listed >= 0
                block = jnp.maximum(listed, 0)
                start = table[base + layout["offset_at"] + source * per_holder + block]
                start = jnp.where(named, start.astype(jnp.int32) - first_row, 0)
                target = jnp.where(named, block, per_holder)
                values = arrived[source * views + view, slot].astype(jnp.float32)
                for z_tile in range(depth_tiles):
                    begin = (target * groups + view * depth_tiles + z_tile) * pitch + start
                    adds.append((begin, values[:, z_tile * LANES : (z_tile + 1) * LANES]))
        held = [placed[pl.ds(begin, rows_dev), :] for begin, _ in adds]
        for (begin, value), old in zip(adds, held):
            placed[pl.ds(begin, rows_dev), :] = old + value
        return carry

    lax.fori_loop(0, bricks, one_source, 0)

    lane = lax.broadcasted_iota(jnp.int32, (groups, LANES), 1)
    own_rows = cores * rows_dev

    def one_row(row, carry):
        for col in range(columns // LANES):
            tiles = [
                placed[pl.ds((col * per_tile + k) * groups * pitch + row, groups, stride=pitch), :]
                for k in range(per_tile)
            ]
            step = per_tile // 2
            while step:
                width = step * layout["block_width"]
                first_half = (lane // width) % 2 == 0
                mixed = list(tiles)
                for k in range(per_tile):
                    if (k // step) % 2 == 0:
                        a, b = tiles[k], tiles[k + step]
                        mixed[k] = jnp.where(first_half, a, pltpu.roll(b, width, 1))
                        mixed[k + step] = jnp.where(first_half, pltpu.roll(a, LANES - width, 1), b)
                tiles = mixed
                step //= 2
            for k, value in enumerate(tiles):
                turned[pl.ds(col * planes + k, groups, stride=per_tile), :] = value
        for col in range(columns // LANES):
            for group in range(planes // SUBLANES):
                measured = turned[pl.ds(col * planes + group * SUBLANES, SUBLANES), :]
                planes_at = pl.ds(group * SUBLANES, SUBLANES)
                field[row + radius, planes_at, pl.ds(col * LANES, LANES)] = (
                    measured * tile(inverse, row, group, col))
        return carry

    lax.fori_loop(0, rows_out, one_row, 0)
    field[0:radius] = jnp.zeros((radius, planes, columns), jnp.float32)
    for target, begin in ((upward, own_rows), (downward, radius)):

        def one_message_row(row, carry):
            target[row] = encode_ratio(field[row + begin], bricks, taps)
            return carry

        lax.fori_loop(0, target.shape[0], one_message_row, 0)


def own_body(layout, field, wx, wy, done):
    rows, planes, columns = done.shape
    lane = lax.broadcasted_iota(jnp.int32, (SUBLANES, LANES), 1)

    def one_row(row, carry):
        for group in range(planes // SUBLANES):
            tiles = blur_row(field, row, group, wx, wy, layout["taps"], True, lane, columns // LANES)
            for col, value in enumerate(tiles):
                done[row, pl.ds(group * SUBLANES, SUBLANES), pl.ds(col * LANES, LANES)] = value
        return carry

    lax.fori_loop(0, rows, one_row, 0, unroll=2)


def rest_body(layout, done, before, after, wx, wy, low, high, keep, send, ahead, behind, total):
    views, part, cores, taps = layout["views"], layout["part"], layout["cores"], layout["taps"]
    bricks = layout["bricks"]
    own_rows, planes, columns = done.shape
    radius = taps // 2
    rows_dev = own_rows // cores
    chip, core, _ = position(cores)
    has_before = (chip > 0).astype(jnp.float32)
    has_after = (chip < bricks // cores - 1).astype(jnp.float32)
    for target, source, mask in ((ahead, before, has_before), (behind, after, has_after)):

        def one_message_row(row, carry):
            target[row] = decode_ratio(source[row], bricks, taps) * mask
            return carry

        lax.fori_loop(0, source.shape[0], one_message_row, 0)
    lane = lax.broadcasted_iota(jnp.int32, (SUBLANES, LANES), 1)
    cols = columns // LANES
    reached = list(range(2 * radius)) + list(range(own_rows - radius, own_rows))

    def one_group(group, carry):
        planes_at = pl.ds(pl.multiple_of(group * SUBLANES, SUBLANES), SUBLANES)
        for row in reached:
            sums = None
            for tap in range(taps):
                at = row + 2 * radius - tap
                if at < 2 * radius:
                    source = ahead
                elif at >= own_rows + radius:
                    source, at = behind, at - own_rows - radius
                else:
                    continue
                weight = wx[tap, planes_at, :]
                terms = [weight * source[at, planes_at, pl.ds(col * LANES, LANES)] for col in range(cols)]
                sums = terms if sums is None else [a + b for a, b in zip(sums, terms)]
            result = [done[row, planes_at, pl.ds(col * LANES, LANES)] for col in range(cols)]
            for tap in range(taps):
                weight = wy[tap, planes_at, :]
                moved = shifted(sums, lane, radius - tap)
                result = [a + weight * m for a, m in zip(result, moved)]
            for col, value in enumerate(result):
                total[row, planes_at, pl.ds(col * LANES, LANES)] = value
        for row in range(own_rows):
            if row not in reached:
                total[row, planes_at, :] = done[row, planes_at, :]
        return carry

    lax.fori_loop(0, planes // SUBLANES, one_group, 0)

    def finish(half, source, target):
        rows = pl.ds(half * rows_dev, rows_dev)
        product = total[rows, 0:part, :]
        for view in range(1, views):
            product = product * total[rows, view * part : (view + 1) * part, :]
        target[...] = source * product

    mine = jnp.where(core == 0, low[...], high[...])
    theirs = jnp.where(core == 0, high[...], low[...])
    finish(core, mine, keep)
    finish(1 - core, theirs, send)


def join_body(keep, near, far, far_near, out, sems):
    _, core, view = position(2)
    part = keep.shape[1]
    copies = []
    for index, (v, c, piece) in enumerate((
        (view, core, keep), (view, 1 - core, near), (1 - view, core, far), (1 - view, 1 - core, far_near))):
        begin = pl.multiple_of((v * 2 + c) * part, part)
        copies.append(pltpu.make_async_copy(piece, out.at[:, pl.ds(begin, part), :], sems.at[index]))
    for copy in copies:
        copy.start()
    for copy in copies:
        copy.wait()


def shards(estimate, camera_blocks, block_lists, block_offsets, psf_index, psf_bank):
    rows_dev, depth, columns = estimate.shape
    _, per_holder, block_rows, block_lanes = camera_blocks.shape
    bricks, slots = block_lists.shape[1], block_lists.shape[3]
    views = lax.axis_size("view")
    kernels, taps = psf_bank.shape[2:]
    radius = taps // 2
    cores = 2
    chips = bricks // cores
    part = depth // (cores * views)
    planes = views * part
    block_width = block_lanes // depth
    brick = lax.axis_index("brick")
    view = lax.axis_index("view")
    core = lax.rem(brick, cores)
    f32 = jnp.float32

    lists = block_lists[0].transpose(0, 2, 1)
    packed = pl.pallas_call(
        pack_body,
        out_shape=pltpu.VMEM(
            (chips, cores, views, slots, block_rows, part * block_width), camera_blocks.dtype),
        in_specs=[SMEM, VMEM],
        out_specs=VMEM,
        compiler_params=GRANT,
        name="pack",
    )(lists, camera_blocks[0])
    packed = packed.reshape(bricks * views, slots, block_rows, part * block_width)
    arrived = lax.all_to_all(packed, ("brick", "view"), 0, 0, tiled=True)

    route = lax.dynamic_index_in_dim(lists, brick - core + cores - 1, 0, keepdims=False)
    pieces = [route.reshape(-1), block_offsets[0], psf_index[0], psf_bank[0].reshape(-1)]
    starts = [0]
    for piece in pieces:
        starts.append(starts[-1] + piece.shape[0])
    length = -(-starts[-1] // LANES) * LANES
    table = jnp.concatenate(
        [piece.astype(f32) for piece in pieces] + [jnp.zeros((length - starts[-1],), f32)])
    if views == 2:
        other = lax.ppermute(table, "view", [(0, 1), (1, 0)])
        table = jnp.concatenate(
            [jnp.where(view == 0, table, other), jnp.where(view == 0, other, table)])
    else:
        table = lax.all_gather(table, "view", tiled=True)
    layout = dict(
        views=views, part=part, cores=cores, taps=taps, kernels=kernels, slots=slots, bricks=bricks,
        per_holder=per_holder, rows_dev=rows_dev, block_width=block_width, table=length,
        offset_at=starts[1], index_at=starts[2], bank_at=starts[3],
        pitch=cores * rows_dev + 2 * radius + 1)

    parts = estimate.reshape(rows_dev, views, cores, part, columns)
    mine = parts[:, view, core]
    theirs = parts[:, view, 1 - core]
    swap = [(i, i ^ 1) for i in range(bricks)]
    up = [(i, i + cores) for i in range(bricks - cores)]
    down = [(i + cores, i) for i in range(bricks - cores)]
    partner = lax.ppermute(theirs, "brick", swap)
    low = jnp.where(core == 0, mine, partner)
    high = jnp.where(core == 0, partner, mine)
    top = lax.ppermute(encode_estimate(high[rows_dev - radius :]), "brick", up)
    bottom = lax.ppermute(encode_estimate(low[: 2 * radius]), "brick", down)

    own_rows = cores * rows_dev
    rows_all = own_rows + radius
    inverse, wx, wy = pl.pallas_call(
        functools.partial(blur_body, layout),
        out_shape=[
            pltpu.VMEM((rows_all, planes, columns), f32),
            pltpu.VMEM((taps, planes, LANES), f32),
            pltpu.VMEM((taps, planes, LANES), f32),
        ],
        in_specs=[SMEM] + [VMEM] * 4,
        out_specs=[VMEM] * 3,
        scratch_shapes=[pltpu.VMEM((rows_all + 2 * radius, planes, columns), f32)],
        compiler_params=GRANT,
        name="blur",
    )(table, *near_core(top, low, high, bottom))

    groups = planes * block_width // LANES
    field, upward, downward = pl.pallas_call(
        functools.partial(ratio_body, layout),
        out_shape=[
            pltpu.VMEM((rows_all + radius, planes, columns), f32),
            pltpu.VMEM((2 * radius, planes, columns), jnp.int16),
            pltpu.VMEM((radius, planes, columns), jnp.int16),
        ],
        in_specs=[SMEM, VMEM, VMEM],
        out_specs=[VMEM] * 3,
        scratch_shapes=[
            pltpu.VMEM(((per_holder + 1) * groups * layout["pitch"], LANES), f32),
            pltpu.VMEM((columns // LANES * planes, LANES), f32),
        ],
        compiler_params=GRANT,
        name="ratio",
    )(table, *near_core(arrived, inverse))

    before = lax.ppermute(upward, "brick", up)
    after = lax.ppermute(downward, "brick", down)
    done = pl.pallas_call(
        functools.partial(own_body, layout),
        out_shape=pltpu.VMEM((own_rows, planes, columns), f32),
        in_specs=[VMEM] * 3,
        out_specs=VMEM,
        compiler_params=GRANT,
        name="own",
    )(*near_core(field, wx, wy))
    piece = pltpu.VMEM((rows_dev, part, columns), f32)
    keep, send = pl.pallas_call(
        functools.partial(rest_body, layout),
        out_shape=[piece, piece],
        in_specs=[VMEM] * 7,
        out_specs=[VMEM] * 2,
        scratch_shapes=[
            pltpu.VMEM((2 * radius, planes, columns), f32),
            pltpu.VMEM((radius, planes, columns), f32),
            pltpu.VMEM((own_rows, planes, columns), f32),
        ],
        compiler_params=GRANT,
        name="rest",
    )(*near_core(done, before, after, wx, wy, low, high))

    if views == 2:
        turn = [(0, 1), (1, 0)]
        far = lax.ppermute(keep, "view", turn)
        near = lax.ppermute(send, "brick", swap)
        far_near = lax.ppermute(near, "view", turn)
        return pl.pallas_call(
            join_body,
            out_shape=jax.ShapeDtypeStruct(estimate.shape, f32),
            in_specs=[VMEM] * 4,
            out_specs=HBM,
            scratch_shapes=[pltpu.SemaphoreType.DMA((4,))],
            compiler_params=GRANT,
            name="join",
        )(*near_core(keep, near, far, far_near))
    near = lax.ppermute(send, "brick", swap)
    both = jnp.stack([jnp.where(core == 0, keep, near), jnp.where(core == 0, near, keep)], axis=1)
    everything = lax.all_gather(both, "view")
    return everything.transpose(1, 0, 2, 3, 4).reshape(estimate.shape)


def solution(mesh):
    placed = (
        P("brick", None, None),
        P("view", "brick", None, None),
        P("view", None, None, None),
        P("view", None),
        P("view", None),
        P("view", None, None, None),
    )
    return jax.shard_map(
        shards, mesh=mesh, in_specs=placed, out_specs=P("brick", None, None), check_vma=False
    )
```

```python
import functools
import math

import jax
import jax.numpy as jnp
from jax import lax
from jax.experimental import pallas as pl
from jax.experimental.pallas import tpu as pltpu
from jax.sharding import PartitionSpec as P


CAMERA = (0.099609375, 2.0)
PSF = (0.03, 0.3)
ESTIMATE = (0.5, 2.0)
CODE_TOP = 32767.0
SCALE_STEPS = 64.0
TINY = 1e-35
LANES = 128
SUBLANES = 8
GRANT = pltpu.CompilerParams(vmem_limit_bytes=12 << 20)
VMEM = pl.BlockSpec(memory_space=pltpu.VMEM)
HBM = pl.BlockSpec(memory_space=pl.ANY)
SMEM = pl.BlockSpec(memory_space=pltpu.SMEM)


def tile(ref, row, group, col):
    return ref[row, pl.ds(group * SUBLANES, SUBLANES), pl.ds(col * LANES, LANES)]


def shifted(tiles, lane, shift):
    if shift == 0:
        return tiles
    zero = jnp.zeros_like(tiles[0])
    rolled = [pltpu.roll(t, (-shift) % LANES, 1) for t in tiles]
    if shift > 0:
        ahead = rolled[1:] + [zero]
        return [jnp.where(lane < LANES - shift, a, b) for a, b in zip(rolled, ahead)]
    behind = [zero] + rolled[:-1]
    return [jnp.where(lane >= -shift, a, b) for a, b in zip(rolled, behind)]


def blur_row(source, row, group, wx, wy, taps, reverse, lane, cols):
    radius = taps // 2
    planes = pl.ds(group * SUBLANES, SUBLANES)
    sums = None
    for tap in range(taps):
        at = row + (2 * radius - tap if reverse else tap)
        weight = wx[tap, planes, :]
        terms = [weight * tile(source, at, group, col) for col in range(cols)]
        sums = terms if sums is None else [a + b for a, b in zip(sums, terms)]
    result = None
    for tap in range(taps):
        weight = wy[tap, planes, :]
        moved = shifted(sums, lane, radius - tap if reverse else tap - radius)
        terms = [weight * m for m in moved]
        result = terms if result is None else [a + b for a, b in zip(result, terms)]
    return result


def near_core(*values):
    return [pltpu.with_memory_space_constraint(value, pltpu.VMEM) for value in values]


def far_memory(*values):
    return [pltpu.with_memory_space_constraint(value, pltpu.HBM) for value in values]


def position(cores):
    brick = lax.axis_index("brick")
    return lax.div(brick, cores), lax.rem(brick, cores), lax.axis_index("view")


def ratio_range(bricks, taps):
    least = CAMERA[0] / (taps * taps * PSF[1] * PSF[1] * ESTIMATE[1])
    inside = taps // 2 + 1
    most = bricks * CAMERA[1] / (inside * inside * PSF[0] * PSF[0] * ESTIMATE[0])
    low, high = math.log(least) - 0.01, math.log(most) + 0.01
    return low, (high - low) / (2 * CODE_TOP - 1)


def encode_ratio(value, bricks, taps):
    low, step = ratio_range(bricks, taps)
    tiny = math.exp(low)
    code = jnp.round((jnp.log(jnp.maximum(value, tiny)) - low) * (1.0 / step)) + (1.0 - CODE_TOP)
    code = jnp.where(value > 0, jnp.minimum(code, CODE_TOP), -CODE_TOP)
    return code.astype(jnp.int32).astype(jnp.int16)


def decode_ratio(code, bricks, taps):
    low, step = ratio_range(bricks, taps)
    code = code.astype(jnp.int32).astype(jnp.float32)
    value = jnp.exp((code + (CODE_TOP - 1.0)) * step + low)
    return jnp.where(code > -CODE_TOP, value, 0.0)


def encode_estimate(value):
    scale = 2 * CODE_TOP / (ESTIMATE[1] - ESTIMATE[0])
    code = jnp.round((value - ESTIMATE[0]) * scale) - CODE_TOP
    return code.astype(jnp.int32).astype(jnp.int16)


def decode_estimate(code):
    scale = (ESTIMATE[1] - ESTIMATE[0]) / (2 * CODE_TOP)
    return (code.astype(jnp.int32).astype(jnp.float32) + CODE_TOP) * scale + ESTIMATE[0]


def encode_rows(value):
    most = jnp.maximum(jnp.max(value, axis=-1, keepdims=True), TINY)
    level = jnp.ceil(jnp.log(most) * (SCALE_STEPS / math.log(2.0))) + 1.0
    factor = jnp.exp(level * (-math.log(2.0) / SCALE_STEPS)) * (2 * CODE_TOP)
    code = jnp.minimum(jnp.round(value * factor), 2 * CODE_TOP) - CODE_TOP
    return code.astype(jnp.int32).astype(jnp.int16), level


def decode_row(code, levels, row):
    levels = levels[:, row : row + 1].astype(jnp.int32).astype(jnp.float32)
    factor = jnp.exp(levels * (math.log(2.0) / SCALE_STEPS)) * (1.0 / (2 * CODE_TOP))
    return (code.astype(jnp.int32).astype(jnp.float32) + CODE_TOP) * factor


def pack_body(listed, blocks, estimate, out, edges, mine, theirs, held, lists, sems):
    chips, cores, views, slots, _, width = out.shape
    here = lax.axis_index("brick")
    _, core, view = position(cores)
    part = mine.shape[1]
    copies = [
        pltpu.make_async_copy(blocks, held, sems.at[0]),
        pltpu.make_async_copy(listed, lists, sems.at[3]),
    ]
    for index, (half, target) in enumerate(((core, mine), (1 - core, theirs))):
        begin = pl.multiple_of((view * cores + half) * part, part)
        copies.append(pltpu.make_async_copy(
            estimate.at[:, pl.ds(begin, part), :], target, sems.at[1 + index]))
    for copy in reversed(copies):
        copy.start()
    copies[2].wait()
    edges[core] = encode_estimate(mine[...])
    copies[3].wait()
    edges[1 - core] = encode_estimate(theirs[...])
    copies[1].wait()
    copies[0].wait()

    def one_chip(chip, carry):
        for slot in range(slots):
            block = jnp.maximum(lists[cores * chip + cores - 1, slot, here], 0)
            for half in range(cores):
                for other in range(views):
                    begin = (other * cores + half) * width
                    out[chip, half, other, slot] = held[block, :, begin : begin + width]
        return carry

    lax.fori_loop(0, chips, one_chip, 0, unroll=2)


def blur_body(layout, table, mine, partner, across, passed, inverse, wx, wy, field):
    views, part, cores, taps, kernels = (
        layout["views"], layout["part"], layout["cores"], layout["taps"], layout["kernels"])
    chip, core, view_here = position(cores)
    where = view_here * cores + core
    has_top = (chip > 0).astype(jnp.float32)
    has_bottom = (chip < layout["bricks"] // cores - 1).astype(jnp.float32)
    first = core == 0
    radius = taps // 2
    direct = decode_estimate(across[core])
    relayed = decode_estimate(passed[...])
    rows = (jnp.where(first, direct, relayed)[mine.shape[0] - radius :] * has_top,
            jnp.where(first, mine[...], partner[...]), jnp.where(first, partner[...], mine[...]),
            jnp.where(first, relayed, direct)[: 2 * radius] * has_bottom)
    for view in range(views):
        base = view * layout["table"]

        def one_plane(plane, carry):
            pick = table[base + layout["index_at"] + where * part + plane].astype(jnp.int32)
            for axis, target in enumerate((wx, wy)):
                begin = base + layout["bank_at"] + (axis * kernels + pick) * taps
                for tap in range(taps):
                    target[tap, pl.ds(view * part + plane, 1), :] = jnp.full(
                        (1, LANES), table[begin + tap], jnp.float32)
            return carry

        lax.fori_loop(0, part, one_plane, 0)
        planes = slice(view * part, (view + 1) * part)
        at = 0
        for piece in rows:
            field[at : at + piece.shape[0], planes, :] = piece
            at += piece.shape[0]
    rows_out, planes, columns = inverse.shape
    own_rows = cores * layout["rows_dev"]
    lane = lax.broadcasted_iota(jnp.int32, (SUBLANES, LANES), 1)

    def one_row(row, carry):
        wanted = jnp.where(row < own_rows, 1.0, has_bottom)
        for group in range(planes // SUBLANES):
            tiles = blur_row(field, row, group, wx, wy, taps, False, lane, columns // LANES)
            for col, value in enumerate(tiles):
                inverse[row, pl.ds(group * SUBLANES, SUBLANES), pl.ds(col * LANES, LANES)] = wanted / value
        return carry

    lax.fori_loop(0, rows_out, one_row, 0, unroll=2)


def ratio_body(layout, table, arrived, inverse, field, upward, downward, placed, turned):
    views, cores, slots, taps = layout["views"], layout["cores"], layout["slots"], layout["taps"]
    bricks, per_holder, rows_dev = layout["bricks"], layout["per_holder"], layout["rows_dev"]
    rows_out, planes, columns = inverse.shape
    radius = taps // 2
    per_tile = LANES // layout["block_width"]
    depth_tiles = layout["part"] // per_tile
    groups = views * depth_tiles
    pitch = layout["pitch"]
    chip, _, _ = position(cores)
    first_row = chip * cores * rows_dev
    placed[...] = jnp.zeros_like(placed)

    def one_source(source, carry):
        adds = []
        for view in range(views):
            base = view * layout["table"]
            for slot in range(slots):
                listed = table[base + slot * bricks + source].astype(jnp.int32)
                named = listed >= 0
                block = jnp.maximum(listed, 0)
                start = table[base + layout["offset_at"] + source * per_holder + block]
                start = jnp.where(named, start.astype(jnp.int32) - first_row, 0)
                target = jnp.where(named, block, per_holder)
                values = arrived[source * views + view, slot].astype(jnp.float32)
                for z_tile in range(depth_tiles):
                    begin = (target * groups + view * depth_tiles + z_tile) * pitch + start
                    adds.append((begin, values[:, z_tile * LANES : (z_tile + 1) * LANES]))
        held = [placed[pl.ds(begin, rows_dev), :] for begin, _ in adds]
        for (begin, value), old in zip(adds, held):
            placed[pl.ds(begin, rows_dev), :] = old + value
        return carry

    lax.fori_loop(0, bricks, one_source, 0)

    lane = lax.broadcasted_iota(jnp.int32, (groups, LANES), 1)
    own_rows = cores * rows_dev

    def one_row(row, carry):
        for col in range(columns // LANES):
            tiles = [
                placed[pl.ds((col * per_tile + k) * groups * pitch + row, groups, stride=pitch), :]
                for k in range(per_tile)
            ]
            step = per_tile // 2
            while step:
                width = step * layout["block_width"]
                first_half = (lane // width) % 2 == 0
                mixed = list(tiles)
                for k in range(per_tile):
                    if (k // step) % 2 == 0:
                        a, b = tiles[k], tiles[k + step]
                        mixed[k] = jnp.where(first_half, a, pltpu.roll(b, width, 1))
                        mixed[k + step] = jnp.where(first_half, pltpu.roll(a, LANES - width, 1), b)
                tiles = mixed
                step //= 2
            for k, value in enumerate(tiles):
                turned[pl.ds(col * planes + k, groups, stride=per_tile), :] = value
        for col in range(columns // LANES):
            for group in range(planes // SUBLANES):
                measured = turned[pl.ds(col * planes + group * SUBLANES, SUBLANES), :]
                planes_at = pl.ds(group * SUBLANES, SUBLANES)
                field[row + radius, planes_at, pl.ds(col * LANES, LANES)] = (
                    measured * tile(inverse, row, group, col))
        return carry

    lax.fori_loop(0, rows_out, one_row, 0)
    field[0:radius] = jnp.zeros((radius, planes, columns), jnp.float32)
    for target, begin in ((upward, own_rows), (downward, radius)):

        def one_message_row(row, carry):
            target[row] = encode_ratio(field[row + begin], bricks, taps)
            return carry

        lax.fori_loop(0, target.shape[0], one_message_row, 0)


def own_body(layout, field, wx, wy, done):
    rows, planes, columns = done.shape
    lane = lax.broadcasted_iota(jnp.int32, (SUBLANES, LANES), 1)

    def one_row(row, carry):
        for group in range(planes // SUBLANES):
            tiles = blur_row(field, row, group, wx, wy, layout["taps"], True, lane, columns // LANES)
            for col, value in enumerate(tiles):
                done[row, pl.ds(group * SUBLANES, SUBLANES), pl.ds(col * LANES, LANES)] = value
        return carry

    lax.fori_loop(0, rows, one_row, 0, unroll=2)


def rest_body(layout, done, before, after, wx, wy, mine, partner, keep, send, ahead, behind, total):
    views, part, cores, taps = layout["views"], layout["part"], layout["cores"], layout["taps"]
    bricks = layout["bricks"]
    own_rows, planes, columns = done.shape
    radius = taps // 2
    rows_dev = own_rows // cores
    chip, core, _ = position(cores)
    has_before = (chip > 0).astype(jnp.float32)
    has_after = (chip < bricks // cores - 1).astype(jnp.float32)
    for target, source, mask in ((ahead, before, has_before), (behind, after, has_after)):

        def one_message_row(row, carry):
            target[row] = decode_ratio(source[row], bricks, taps) * mask
            return carry

        lax.fori_loop(0, source.shape[0], one_message_row, 0)
    lane = lax.broadcasted_iota(jnp.int32, (SUBLANES, LANES), 1)
    cols = columns // LANES
    reached = list(range(2 * radius)) + list(range(own_rows - radius, own_rows))

    def one_group(group, carry):
        planes_at = pl.ds(pl.multiple_of(group * SUBLANES, SUBLANES), SUBLANES)
        for row in reached:
            sums = None
            for tap in range(taps):
                at = row + 2 * radius - tap
                if at < 2 * radius:
                    source = ahead
                elif at >= own_rows + radius:
                    source, at = behind, at - own_rows - radius
                else:
                    continue
                weight = wx[tap, planes_at, :]
                terms = [weight * source[at, planes_at, pl.ds(col * LANES, LANES)] for col in range(cols)]
                sums = terms if sums is None else [a + b for a, b in zip(sums, terms)]
            result = [done[row, planes_at, pl.ds(col * LANES, LANES)] for col in range(cols)]
            for tap in range(taps):
                weight = wy[tap, planes_at, :]
                moved = shifted(sums, lane, radius - tap)
                result = [a + weight * m for a, m in zip(result, moved)]
            for col, value in enumerate(result):
                total[row, planes_at, pl.ds(col * LANES, LANES)] = value
        for row in range(own_rows):
            if row not in reached:
                total[row, planes_at, :] = done[row, planes_at, :]
        return carry

    lax.fori_loop(0, planes // SUBLANES, one_group, 0)

    wide = lax.broadcasted_iota(jnp.int32, (part, LANES), 1)

    def finish(half, source, target):
        def one_row(row, levels):
            at = half * rows_dev + row
            value = source[row]
            for view in range(views):
                value = value * total[at, view * part : (view + 1) * part, :]
            begin = row * columns if isinstance(row, int) else pl.multiple_of(row * columns, LANES)
            target[:, pl.ds(begin, columns)], level = encode_rows(value)
            return jnp.where(wide == row, level, levels)

        levels = lax.fori_loop(
            0, rows_dev, one_row, jnp.zeros((part, LANES), jnp.float32), unroll=True)
        target[:, rows_dev * columns :] = levels.astype(jnp.int32).astype(jnp.int16)

    finish(core, mine, keep)
    finish(1 - core, partner, send)


def join_body(keep, near, far, far_near, out, pieces, sems):
    _, core, view = position(2)
    rows, columns = out.shape[0], out.shape[2]
    part = keep.shape[0]
    copies = []
    for index, (v, c, piece) in enumerate((
        (view, core, keep), (view, 1 - core, near), (1 - view, core, far), (1 - view, 1 - core, far_near))):
        levels = piece[:, rows * columns :]
        for row in range(rows):
            pieces[index, row] = decode_row(
                piece[:, row * columns : (row + 1) * columns], levels, row)
        begin = pl.multiple_of((v * 2 + c) * part, part)
        copies.append(pltpu.make_async_copy(
            pieces.at[index], out.at[:, pl.ds(begin, part), :], sems.at[index]))
        copies[-1].start()
    for copy in copies:
        copy.wait()


def shards(estimate, camera_blocks, block_lists, block_offsets, psf_index, psf_bank):
    rows_dev, depth, columns = estimate.shape
    _, per_holder, block_rows, block_lanes = camera_blocks.shape
    bricks, slots = block_lists.shape[1], block_lists.shape[3]
    views = lax.axis_size("view")
    kernels, taps = psf_bank.shape[2:]
    radius = taps // 2
    cores = 2
    chips = bricks // cores
    part = depth // (cores * views)
    planes = views * part
    block_width = block_lanes // depth
    brick = lax.axis_index("brick")
    view = lax.axis_index("view")
    core = lax.rem(brick, cores)
    f32 = jnp.float32

    lists = block_lists[0].transpose(0, 2, 1)
    outgoing = pltpu.VMEM(
        (chips, cores, views, slots, block_rows, part * block_width), camera_blocks.dtype)
    piece = pltpu.VMEM((rows_dev, part, columns), f32)
    coded = pltpu.VMEM((cores, rows_dev, part, columns), jnp.int16)
    packed, edges, mine, theirs = pl.pallas_call(
        pack_body,
        out_shape=[outgoing, coded, piece, piece],
        in_specs=[HBM] * 3,
        out_specs=[VMEM] * 4,
        scratch_shapes=[
            pltpu.VMEM(camera_blocks.shape[1:], camera_blocks.dtype),
            pltpu.SMEM(lists.shape, jnp.int32),
            pltpu.SemaphoreType.DMA((4,)),
        ],
        compiler_params=GRANT,
        name="pack",
    )(*far_memory(lists, camera_blocks[0], estimate))
    swap = [(i, i ^ 1) for i in range(bricks)]
    packed = packed.reshape(bricks * views, slots, block_rows, part * block_width)
    across = lax.ppermute(edges, "brick", [
        (i, j) for i in range(bricks) for j in [i + 1 if i % cores else i - 1]
        if 0 <= j < bricks])
    partner = lax.ppermute(theirs, "brick", swap)
    arrived = lax.all_to_all(packed, ("brick", "view"), 0, 0, tiled=True)

    route = lax.dynamic_index_in_dim(lists, brick - core + cores - 1, 0, keepdims=False)
    pieces = [route.reshape(-1), block_offsets[0], psf_index[0], psf_bank[0].reshape(-1)]
    starts = [0]
    for piece in pieces:
        starts.append(starts[-1] + piece.shape[0])
    length = -(-starts[-1] // LANES) * LANES
    table = jnp.concatenate(
        [piece.astype(f32) for piece in pieces] + [jnp.zeros((length - starts[-1],), f32)])
    if views == 2:
        other = lax.ppermute(table, "view", [(0, 1), (1, 0)])
    layout = dict(
        views=views, part=part, cores=cores, taps=taps, kernels=kernels, slots=slots, bricks=bricks,
        per_holder=per_holder, rows_dev=rows_dev, block_width=block_width, table=length,
        offset_at=starts[1], index_at=starts[2], bank_at=starts[3],
        pitch=cores * rows_dev + 2 * radius + 1)

    up = [(i, i + cores) for i in range(bricks - cores)]
    down = [(i + cores, i) for i in range(bricks - cores)]
    passed = lax.ppermute(
        lax.dynamic_index_in_dim(across, 1 - core, 0, keepdims=False), "brick", swap)
    if views == 2:
        table = jnp.concatenate(
            [jnp.where(view == 0, table, other), jnp.where(view == 0, other, table)])
    else:
        table = lax.all_gather(table, "view", tiled=True)

    own_rows = cores * rows_dev
    rows_all = own_rows + radius
    inverse, wx, wy = pl.pallas_call(
        functools.partial(blur_body, layout),
        out_shape=[
            pltpu.VMEM((rows_all, planes, columns), f32),
            pltpu.VMEM((taps, planes, LANES), f32),
            pltpu.VMEM((taps, planes, LANES), f32),
        ],
        in_specs=[SMEM] + [VMEM] * 4,
        out_specs=[VMEM] * 3,
        scratch_shapes=[pltpu.VMEM((rows_all + 2 * radius, planes, columns), f32)],
        compiler_params=GRANT,
        name="blur",
    )(table, *near_core(mine, partner, across, passed))

    groups = planes * block_width // LANES
    field, upward, downward = pl.pallas_call(
        functools.partial(ratio_body, layout),
        out_shape=[
            pltpu.VMEM((rows_all + radius, planes, columns), f32),
            pltpu.VMEM((2 * radius, planes, columns), jnp.int16),
            pltpu.VMEM((radius, planes, columns), jnp.int16),
        ],
        in_specs=[SMEM, VMEM, VMEM],
        out_specs=[VMEM] * 3,
        scratch_shapes=[
            pltpu.VMEM(((per_holder + 1) * groups * layout["pitch"], LANES), f32),
            pltpu.VMEM((columns // LANES * planes, LANES), f32),
        ],
        compiler_params=GRANT,
        name="ratio",
    )(table, *near_core(arrived, inverse))

    before = lax.ppermute(upward, "brick", up)
    after = lax.ppermute(downward, "brick", down)
    done = pl.pallas_call(
        functools.partial(own_body, layout),
        out_shape=pltpu.VMEM((own_rows, planes, columns), f32),
        in_specs=[VMEM] * 3,
        out_specs=VMEM,
        compiler_params=GRANT,
        name="own",
    )(*near_core(field, wx, wy))
    piece = pltpu.VMEM((part, rows_dev * columns + LANES), jnp.int16)
    keep, send = pl.pallas_call(
        functools.partial(rest_body, layout),
        out_shape=[piece, piece],
        in_specs=[VMEM] * 7,
        out_specs=[VMEM] * 2,
        scratch_shapes=[
            pltpu.VMEM((2 * radius, planes, columns), f32),
            pltpu.VMEM((radius, planes, columns), f32),
            pltpu.VMEM((own_rows, planes, columns), f32),
        ],
        compiler_params=GRANT,
        name="rest",
    )(*near_core(done, before, after, wx, wy, mine, partner))

    if views == 2:
        turn = [(0, 1), (1, 0)]
        far = lax.ppermute(keep, "view", turn)
        near = lax.ppermute(send, "brick", swap)
        far_near = lax.ppermute(near, "view", turn)
        return pl.pallas_call(
            join_body,
            out_shape=jax.ShapeDtypeStruct(estimate.shape, f32),
            in_specs=[VMEM] * 4,
            out_specs=HBM,
            scratch_shapes=[
                pltpu.VMEM((4, rows_dev, part, columns), f32), pltpu.SemaphoreType.DMA((4,))],
            compiler_params=GRANT,
            name="join",
        )(*near_core(keep, near, far, far_near))
    near = lax.ppermute(send, "brick", swap)
    both = jnp.stack([jnp.where(core == 0, keep, near), jnp.where(core == 0, near, keep)])
    coded = lax.all_gather(both, "view").reshape((-1,) + keep.shape)
    rows = [
        jax.vmap(lambda piece, row=row: decode_row(
            piece[:, row * columns : (row + 1) * columns], piece[:, rows_dev * columns :], row))(coded)
        for row in range(rows_dev)
    ]
    return jnp.stack(rows).reshape(estimate.shape)


def solution(mesh):
    placed = (
        P("brick", None, None),
        P("view", "brick", None, None),
        P("view", None, None, None),
        P("view", None),
        P("view", None),
        P("view", None, None, None),
    )
    return jax.shard_map(
        shards, mesh=mesh, in_specs=placed, out_specs=P("brick", None, None), check_vma=False
    )
```

```python
import functools
import math

import jax
import jax.numpy as jnp
from jax import lax
from jax.experimental import pallas as pl
from jax.experimental.pallas import tpu as pltpu
from jax.sharding import PartitionSpec as P


CAMERA = (0.099609375, 2.0)
PSF = (0.03, 0.3)
ESTIMATE = (0.5, 2.0)
CODE_TOP = 32767.0
SCALE_STEPS = 64.0
TINY = 1e-35
LANES = 128
SUBLANES = 8
UNROLL = 4
GRANT = pltpu.CompilerParams(vmem_limit_bytes=12 << 20)
VMEM = pl.BlockSpec(memory_space=pltpu.VMEM)
HBM = pl.BlockSpec(memory_space=pl.ANY)
SMEM = pl.BlockSpec(memory_space=pltpu.SMEM)


def tile(ref, row, group, col):
    return ref[row, pl.ds(group * SUBLANES, SUBLANES), pl.ds(col * LANES, LANES)]


def shifted(tiles, lane, shift):
    if shift == 0:
        return tiles
    zero = jnp.zeros_like(tiles[0])
    rolled = [pltpu.roll(t, (-shift) % LANES, 1) for t in tiles]
    if shift > 0:
        ahead = rolled[1:] + [zero]
        return [jnp.where(lane < LANES - shift, a, b) for a, b in zip(rolled, ahead)]
    behind = [zero] + rolled[:-1]
    return [jnp.where(lane >= -shift, a, b) for a, b in zip(rolled, behind)]


def blur_row(source, row, group, wx, wy, taps, reverse, lane, cols):
    radius = taps // 2
    planes = pl.ds(group * SUBLANES, SUBLANES)
    sums = None
    for tap in range(taps):
        at = row + (2 * radius - tap if reverse else tap)
        weight = wx[tap, planes, :]
        terms = [weight * tile(source, at, group, col) for col in range(cols)]
        sums = terms if sums is None else [a + b for a, b in zip(sums, terms)]
    result = None
    for tap in range(taps):
        weight = wy[tap, planes, :]
        moved = shifted(sums, lane, radius - tap if reverse else tap - radius)
        terms = [weight * m for m in moved]
        result = terms if result is None else [a + b for a, b in zip(result, terms)]
    return result


def near_core(*values):
    return [pltpu.with_memory_space_constraint(value, pltpu.VMEM) for value in values]


def far_memory(*values):
    return [pltpu.with_memory_space_constraint(value, pltpu.HBM) for value in values]


def position(cores):
    brick = lax.axis_index("brick")
    return lax.div(brick, cores), lax.rem(brick, cores), lax.axis_index("view")


def ratio_range(bricks, taps):
    least = CAMERA[0] / (taps * taps * PSF[1] * PSF[1] * ESTIMATE[1])
    inside = taps // 2 + 1
    most = bricks * CAMERA[1] / (inside * inside * PSF[0] * PSF[0] * ESTIMATE[0])
    low, high = math.log(least) - 0.01, math.log(most) + 0.01
    return low, (high - low) / (2 * CODE_TOP - 1)


def encode_ratio(value, bricks, taps):
    low, step = ratio_range(bricks, taps)
    tiny = math.exp(low)
    code = jnp.round((jnp.log(jnp.maximum(value, tiny)) - low) * (1.0 / step)) + (1.0 - CODE_TOP)
    code = jnp.where(value > 0, jnp.minimum(code, CODE_TOP), -CODE_TOP)
    return code.astype(jnp.int32).astype(jnp.int16)


def decode_ratio(code, bricks, taps):
    low, step = ratio_range(bricks, taps)
    code = code.astype(jnp.int32).astype(jnp.float32)
    value = jnp.exp((code + (CODE_TOP - 1.0)) * step + low)
    return jnp.where(code > -CODE_TOP, value, 0.0)


def encode_estimate(value):
    scale = 2 * CODE_TOP / (ESTIMATE[1] - ESTIMATE[0])
    code = jnp.round((value - ESTIMATE[0]) * scale) - CODE_TOP
    return code.astype(jnp.int32).astype(jnp.int16)


def decode_estimate(code):
    scale = (ESTIMATE[1] - ESTIMATE[0]) / (2 * CODE_TOP)
    return (code.astype(jnp.int32).astype(jnp.float32) + CODE_TOP) * scale + ESTIMATE[0]


def encode_rows(value):
    most = jnp.maximum(jnp.max(value, axis=-1, keepdims=True), TINY)
    level = jnp.ceil(jnp.log(most) * (SCALE_STEPS / math.log(2.0))) + 1.0
    factor = jnp.exp(level * (-math.log(2.0) / SCALE_STEPS)) * (2 * CODE_TOP)
    code = jnp.minimum(jnp.round(value * factor), 2 * CODE_TOP) - CODE_TOP
    return code.astype(jnp.int32).astype(jnp.int16), level


def decode_row(code, levels, row):
    levels = levels[:, row : row + 1].astype(jnp.int32).astype(jnp.float32)
    factor = jnp.exp(levels * (math.log(2.0) / SCALE_STEPS)) * (1.0 / (2 * CODE_TOP))
    return (code.astype(jnp.int32).astype(jnp.float32) + CODE_TOP) * factor


def pack_body(listed, blocks, estimate, out, edges, mine, theirs, held, lists, sems):
    chips, cores, views, slots, _, width = out.shape
    here = lax.axis_index("brick")
    _, core, view = position(cores)
    part = mine.shape[1]
    copies = [
        pltpu.make_async_copy(blocks, held, sems.at[0]),
        pltpu.make_async_copy(listed, lists, sems.at[3]),
    ]
    for index, (half, target) in enumerate(((core, mine), (1 - core, theirs))):
        begin = pl.multiple_of((view * cores + half) * part, part)
        copies.append(pltpu.make_async_copy(
            estimate.at[:, pl.ds(begin, part), :], target, sems.at[1 + index]))
    for copy in reversed(copies):
        copy.start()
    copies[2].wait()
    edges[core] = encode_estimate(mine[...])
    copies[3].wait()
    edges[1 - core] = encode_estimate(theirs[...])
    copies[1].wait()
    copies[0].wait()

    def one_chip(chip, carry):
        for slot in range(slots):
            block = jnp.maximum(lists[cores * chip + cores - 1, slot, here], 0)
            for half in range(cores):
                for other in range(views):
                    begin = (other * cores + half) * width
                    out[chip, half, other, slot] = held[block, :, begin : begin + width]
        return carry

    lax.fori_loop(0, chips, one_chip, 0, unroll=2)


def blur_body(layout, table, mine, partner, across, passed, inverse, wx, wy, cleared, field):
    views, part, cores, taps, kernels = (
        layout["views"], layout["part"], layout["cores"], layout["taps"], layout["kernels"])
    chip, core, view_here = position(cores)
    where = view_here * cores + core
    has_top = (chip > 0).astype(jnp.float32)
    has_bottom = (chip < layout["bricks"] // cores - 1).astype(jnp.float32)
    first = core == 0
    radius = taps // 2
    direct = decode_estimate(across[core])
    relayed = decode_estimate(passed[...])
    rows = (jnp.where(first, direct, relayed)[mine.shape[0] - radius :] * has_top,
            jnp.where(first, mine[...], partner[...]), jnp.where(first, partner[...], mine[...]),
            jnp.where(first, relayed, direct)[: 2 * radius] * has_bottom)
    for view in range(views):
        base = view * layout["table"]

        def one_plane(plane, carry):
            pick = table[base + layout["index_at"] + where * part + plane].astype(jnp.int32)
            for axis, target in enumerate((wx, wy)):
                begin = base + layout["bank_at"] + (axis * kernels + pick) * taps
                for tap in range(taps):
                    target[tap, pl.ds(view * part + plane, 1), :] = jnp.full(
                        (1, LANES), table[begin + tap], jnp.float32)
            return carry

        lax.fori_loop(0, part, one_plane, 0)
        planes = slice(view * part, (view + 1) * part)
        at = 0
        for piece in rows:
            field[at : at + piece.shape[0], planes, :] = piece
            at += piece.shape[0]
    rows_out, planes, columns = inverse.shape
    cleared[...] = jnp.zeros_like(cleared)
    own_rows = cores * layout["rows_dev"]
    lane = lax.broadcasted_iota(jnp.int32, (SUBLANES, LANES), 1)

    def one_row(row, carry):
        wanted = jnp.where(row < own_rows, 1.0, has_bottom)
        for group in range(planes // SUBLANES):
            tiles = blur_row(field, row, group, wx, wy, taps, False, lane, columns // LANES)
            for col, value in enumerate(tiles):
                inverse[row, pl.ds(group * SUBLANES, SUBLANES), pl.ds(col * LANES, LANES)] = wanted / value
        return carry

    lax.fori_loop(0, rows_out, one_row, 0, unroll=2)


def ratio_row(layout, placed, inverse, field, turned, row):
    _, planes, columns = field.shape
    radius = layout["taps"] // 2
    block_width, pitch = layout["block_width"], layout["pitch"]
    per_tile = LANES // block_width
    groups = planes // per_tile
    lane = lax.broadcasted_iota(jnp.int32, (groups, LANES), 1)
    for col in range(columns // LANES):
        tiles = [
            placed[pl.ds((col * per_tile + k) * groups * pitch + row, groups, stride=pitch), :]
            for k in range(per_tile)
        ]
        step = per_tile // 2
        while step:
            width = step * block_width
            first_half = (lane // width) % 2 == 0
            mixed = list(tiles)
            for k in range(per_tile):
                if (k // step) % 2 == 0:
                    a, b = tiles[k], tiles[k + step]
                    mixed[k] = jnp.where(first_half, a, pltpu.roll(b, width, 1))
                    mixed[k + step] = jnp.where(first_half, pltpu.roll(a, LANES - width, 1), b)
            tiles = mixed
            step //= 2
        for k, value in enumerate(tiles):
            turned[pl.ds(col * planes + k, groups, stride=per_tile), :] = value
    for col in range(columns // LANES):
        for group in range(planes // SUBLANES):
            measured = turned[pl.ds(col * planes + group * SUBLANES, SUBLANES), :]
            planes_at = pl.ds(group * SUBLANES, SUBLANES)
            field[row + radius, planes_at, pl.ds(col * LANES, LANES)] = (
                measured * tile(inverse, row, group, col))


def ratio_body(layout, table, arrived, inverse, cleared, placed, field, upward, downward, turned):
    views, cores, slots, taps = layout["views"], layout["cores"], layout["slots"], layout["taps"]
    bricks, per_holder, rows_dev = layout["bricks"], layout["per_holder"], layout["rows_dev"]
    radius = taps // 2
    per_tile = LANES // layout["block_width"]
    depth_tiles = layout["part"] // per_tile
    groups = views * depth_tiles
    pitch = layout["pitch"]
    chip, _, _ = position(cores)
    first_row = chip * cores * rows_dev

    def one_source(source, carry):
        adds = []
        for view in range(views):
            base = view * layout["table"]
            for slot in range(slots):
                listed = table[base + slot * bricks + source].astype(jnp.int32)
                named = listed >= 0
                block = jnp.maximum(listed, 0)
                start = table[base + layout["offset_at"] + source * per_holder + block]
                start = jnp.where(named, start.astype(jnp.int32) - first_row, 0)
                target = jnp.where(named, block, per_holder)
                values = arrived[source * views + view, slot].astype(jnp.float32)
                for z_tile in range(depth_tiles):
                    begin = (target * groups + view * depth_tiles + z_tile) * pitch + start
                    adds.append((begin, values[:, z_tile * LANES : (z_tile + 1) * LANES]))
        held = [placed[pl.ds(begin, rows_dev), :] for begin, _ in adds]
        for (begin, value), old in zip(adds, held):
            placed[pl.ds(begin, rows_dev), :] = old + value
        return carry

    lax.fori_loop(0, bricks, one_source, 0, unroll=UNROLL)

    own_rows = cores * rows_dev
    for target, begin in ((upward, own_rows - radius), (downward, 0)):

        def one_row(row, carry):
            ratio_row(layout, placed, inverse, field, turned, row + begin)
            target[row] = encode_ratio(field[row + begin + radius], bricks, taps)
            return carry

        lax.fori_loop(0, target.shape[0], one_row, 0, unroll=2)


def own_body(layout, placed, inverse, edges, wx, wy, field, done, turned):
    rows, planes, columns = done.shape
    radius = layout["taps"] // 2
    lane = lax.broadcasted_iota(jnp.int32, (SUBLANES, LANES), 1)
    field[0:radius] = jnp.zeros((radius, planes, columns), jnp.float32)

    def inner_row(row, carry):
        ratio_row(layout, placed, inverse, field, turned, row)
        return carry

    lax.fori_loop(radius, rows - radius, inner_row, 0)

    def one_row(row, carry):
        for group in range(planes // SUBLANES):
            tiles = blur_row(field, row, group, wx, wy, layout["taps"], True, lane, columns // LANES)
            for col, value in enumerate(tiles):
                done[row, pl.ds(group * SUBLANES, SUBLANES), pl.ds(col * LANES, LANES)] = value
        return carry

    lax.fori_loop(0, rows, one_row, 0, unroll=2)


def rest_body(layout, flip, done, before, after, wx, wy, source, target, reach, total):
    views, part, cores, taps = layout["views"], layout["part"], layout["cores"], layout["taps"]
    bricks, rows_dev = layout["bricks"], layout["rows_dev"]
    _, planes, columns = done.shape
    radius = taps // 2
    chip, core, _ = position(cores)
    lane = lax.broadcasted_iota(jnp.int32, (SUBLANES, LANES), 1)
    cols = columns // LANES

    def add_received(half):
        message, there = (
            (after, chip < bricks // cores - 1) if half else (before, chip > 0))
        mask = there.astype(jnp.float32)

        def one_message_row(row, carry):
            reach[row] = decode_ratio(message[row], bricks, taps) * mask
            return carry

        lax.fori_loop(0, message.shape[0], one_message_row, 0, unroll=UNROLL)
        first = rows_dev if half else -radius

        def one_group(group, carry):
            planes_at = pl.ds(pl.multiple_of(group * SUBLANES, SUBLANES), SUBLANES)
            for row in range(rows_dev):
                result = [
                    done[half * rows_dev + row, planes_at, pl.ds(col * LANES, LANES)]
                    for col in range(cols)
                ]
                sums = None
                for tap in range(taps):
                    at = row + radius - tap - first
                    if not 0 <= at < message.shape[0]:
                        continue
                    weight = wx[tap, planes_at, :]
                    terms = [
                        weight * reach[at, planes_at, pl.ds(col * LANES, LANES)] for col in range(cols)]
                    sums = terms if sums is None else [a + b for a, b in zip(sums, terms)]
                for tap in range(taps if sums else 0):
                    weight = wy[tap, planes_at, :]
                    moved = shifted(sums, lane, radius - tap)
                    result = [a + weight * m for a, m in zip(result, moved)]
                for col, value in enumerate(result):
                    total[row, planes_at, pl.ds(col * LANES, LANES)] = value
            return carry

        lax.fori_loop(0, planes // SUBLANES, one_group, 0)

    this = 1 - core if flip else core
    for half in range(cores):
        pl.when(this == half)(functools.partial(add_received, half))
    wide = lax.broadcasted_iota(jnp.int32, (part, LANES), 1)
    levels = jnp.zeros((part, LANES), jnp.float32)
    for row in range(rows_dev):
        value = source[row]
        for view in range(views):
            value = value * total[row, view * part : (view + 1) * part, :]
        target[:, row * columns : (row + 1) * columns], level = encode_rows(value)
        levels = jnp.where(wide == row, level, levels)
    target[:, rows_dev * columns :] = levels.astype(jnp.int32).astype(jnp.int16)


def join_body(places, *refs):
    _, core, view = position(2)
    count = len(places)
    sources, (out, held, sems) = refs[:count], refs[-3:]
    rows, columns = out.shape[0], out.shape[2]
    part = sources[0].shape[0]
    copies = []
    for index, (piece, (turn, flip)) in enumerate(zip(sources, places)):
        v = 1 - view if turn else view
        c = 1 - core if flip else core
        levels = piece[:, rows * columns :]
        for row in range(rows):
            held[index, row] = decode_row(piece[:, row * columns : (row + 1) * columns], levels, row)
        begin = pl.multiple_of((v * 2 + c) * part, part)
        copies.append(pltpu.make_async_copy(
            held.at[index], out.at[:, pl.ds(begin, part), :], sems.at[index]))
        copies[-1].start()
    for copy in copies:
        copy.wait()


def join(shape, part, places, pieces, out=None):
    rows, _, columns = shape
    count = len(pieces)
    return pl.pallas_call(
        functools.partial(join_body, places),
        out_shape=jax.ShapeDtypeStruct(shape, jnp.float32),
        in_specs=[VMEM] * count + ([] if out is None else [HBM]),
        out_specs=HBM,
        input_output_aliases={} if out is None else {count: 0},
        scratch_shapes=[
            pltpu.VMEM((count, rows, part, columns), jnp.float32), pltpu.SemaphoreType.DMA((count,))],
        compiler_params=GRANT,
        name="join",
    )(*near_core(*pieces), *([] if out is None else [out]))


def shards(estimate, camera_blocks, block_lists, block_offsets, psf_index, psf_bank):
    rows_dev, depth, columns = estimate.shape
    _, per_holder, block_rows, block_lanes = camera_blocks.shape
    bricks, slots = block_lists.shape[1], block_lists.shape[3]
    views = lax.axis_size("view")
    kernels, taps = psf_bank.shape[2:]
    radius = taps // 2
    cores = 2
    chips = bricks // cores
    part = depth // (cores * views)
    planes = views * part
    block_width = block_lanes // depth
    brick = lax.axis_index("brick")
    view = lax.axis_index("view")
    core = lax.rem(brick, cores)
    f32 = jnp.float32

    lists = block_lists[0].transpose(0, 2, 1)
    outgoing = pltpu.VMEM(
        (chips, cores, views, slots, block_rows, part * block_width), camera_blocks.dtype)
    piece = pltpu.VMEM((rows_dev, part, columns), f32)
    coded = pltpu.VMEM((cores, rows_dev, part, columns), jnp.int16)
    packed, edges, mine, theirs = pl.pallas_call(
        pack_body,
        out_shape=[outgoing, coded, piece, piece],
        in_specs=[HBM] * 3,
        out_specs=[VMEM] * 4,
        scratch_shapes=[
            pltpu.VMEM(camera_blocks.shape[1:], camera_blocks.dtype),
            pltpu.SMEM(lists.shape, jnp.int32),
            pltpu.SemaphoreType.DMA((4,)),
        ],
        compiler_params=GRANT,
        name="pack",
    )(*far_memory(lists, camera_blocks[0], estimate))
    swap = [(i, i ^ 1) for i in range(bricks)]
    packed = packed.reshape(bricks * views, slots, block_rows, part * block_width)
    across = lax.ppermute(edges, "brick", [
        (i, j) for i in range(bricks) for j in [i + 1 if i % cores else i - 1]
        if 0 <= j < bricks])
    partner = lax.ppermute(theirs, "brick", swap)
    arrived = lax.all_to_all(packed, ("brick", "view"), 0, 0, tiled=True)

    route = lax.dynamic_index_in_dim(lists, brick - core + cores - 1, 0, keepdims=False)
    pieces = [route.reshape(-1), block_offsets[0], psf_index[0], psf_bank[0].reshape(-1)]
    starts = [0]
    for piece in pieces:
        starts.append(starts[-1] + piece.shape[0])
    length = -(-starts[-1] // LANES) * LANES
    table = jnp.concatenate(
        [piece.astype(f32) for piece in pieces] + [jnp.zeros((length - starts[-1],), f32)])
    if views == 2:
        other = lax.ppermute(table, "view", [(0, 1), (1, 0)])
    layout = dict(
        views=views, part=part, cores=cores, taps=taps, kernels=kernels, slots=slots, bricks=bricks,
        per_holder=per_holder, rows_dev=rows_dev, block_width=block_width, table=length,
        offset_at=starts[1], index_at=starts[2], bank_at=starts[3],
        pitch=cores * rows_dev + 2 * radius + 1)

    up = [(i, i + cores) for i in range(bricks - cores)]
    down = [(i + cores, i) for i in range(bricks - cores)]
    passed = lax.ppermute(
        lax.dynamic_index_in_dim(across, 1 - core, 0, keepdims=False), "brick", swap)
    if views == 2:
        table = jnp.concatenate(
            [jnp.where(view == 0, table, other), jnp.where(view == 0, other, table)])
    else:
        table = lax.all_gather(table, "view", tiled=True)

    own_rows = cores * rows_dev
    rows_all = own_rows + radius
    groups = planes * block_width // LANES
    placing = pltpu.VMEM(((per_holder + 1) * groups * layout["pitch"], LANES), f32)
    inverse, wx, wy, cleared = pl.pallas_call(
        functools.partial(blur_body, layout),
        out_shape=[
            pltpu.VMEM((rows_all, planes, columns), f32),
            pltpu.VMEM((taps, planes, LANES), f32),
            pltpu.VMEM((taps, planes, LANES), f32),
            placing,
        ],
        in_specs=[SMEM] + [VMEM] * 4,
        out_specs=[VMEM] * 4,
        scratch_shapes=[pltpu.VMEM((rows_all + 2 * radius, planes, columns), f32)],
        compiler_params=GRANT,
        name="blur",
    )(table, *near_core(mine, partner, across, passed))

    edged = pltpu.VMEM((rows_all + radius, planes, columns), f32)
    turning = pltpu.VMEM((columns // LANES * planes, LANES), f32)
    placed, field, upward, downward = pl.pallas_call(
        functools.partial(ratio_body, layout),
        out_shape=[
            placing,
            edged,
            pltpu.VMEM((2 * radius, planes, columns), jnp.int16),
            pltpu.VMEM((radius, planes, columns), jnp.int16),
        ],
        in_specs=[SMEM] + [VMEM] * 3,
        out_specs=[VMEM] * 4,
        input_output_aliases={3: 0},
        scratch_shapes=[turning],
        compiler_params=GRANT,
        name="ratio",
    )(table, *near_core(arrived, inverse, cleared))

    before = lax.ppermute(upward, "brick", up)
    after = lax.ppermute(downward, "brick", down)
    _, done = pl.pallas_call(
        functools.partial(own_body, layout),
        out_shape=[edged, pltpu.VMEM((own_rows, planes, columns), f32)],
        in_specs=[VMEM] * 5,
        out_specs=[VMEM] * 2,
        input_output_aliases={2: 0},
        scratch_shapes=[turning],
        compiler_params=GRANT,
        name="own",
    )(*near_core(placed, inverse, field, wx, wy))

    def finished(flip, source):
        return pl.pallas_call(
            functools.partial(rest_body, layout, flip),
            out_shape=pltpu.VMEM((part, rows_dev * columns + LANES), jnp.int16),
            in_specs=[VMEM] * 6,
            out_specs=VMEM,
            scratch_shapes=[
                pltpu.VMEM((2 * radius, planes, columns), f32),
                pltpu.VMEM((rows_dev, planes, columns), f32),
            ],
            compiler_params=GRANT,
            name="rest",
        )(*near_core(done, before, after, wx, wy, source))

    if views == 2:
        turn = [(0, 1), (1, 0)]
        keep = finished(False, mine)
        far = lax.ppermute(keep, "view", turn)
        send = finished(True, partner)
        near = lax.ppermute(send, "brick", swap)
        far_near = lax.ppermute(near, "view", turn)
        out = join(estimate.shape, part, ((False, False), (False, True)), (keep, near))
        out = join(estimate.shape, part, ((True, False),), (far,), out)
        return join(estimate.shape, part, ((True, True),), (far_near,), out)
    keep = finished(False, mine)
    near = lax.ppermute(finished(True, partner), "brick", swap)
    both = jnp.stack([jnp.where(core == 0, keep, near), jnp.where(core == 0, near, keep)])
    coded = lax.all_gather(both, "view").reshape((-1,) + keep.shape)
    rows = [
        jax.vmap(lambda piece, row=row: decode_row(
            piece[:, row * columns : (row + 1) * columns], piece[:, rows_dev * columns :], row))(coded)
        for row in range(rows_dev)
    ]
    return jnp.stack(rows).reshape(estimate.shape)


def solution(mesh):
    placed = (
        P("brick", None, None),
        P("view", "brick", None, None),
        P("view", None, None, None),
        P("view", None),
        P("view", None),
        P("view", None, None, None),
    )
    return jax.shard_map(
        shards, mesh=mesh, in_specs=placed, out_specs=P("brick", None, None), check_vma=False
    )
```

```python
import functools
import math

import jax
import jax.numpy as jnp
from jax import lax
from jax.experimental import pallas as pl
from jax.experimental.pallas import tpu as pltpu
from jax.sharding import PartitionSpec as P


CAMERA = (0.099609375, 2.0)
PSF = (0.03, 0.3)
ESTIMATE = (0.5, 2.0)
CODE_TOP = 32767.0
SCALE_STEPS = 64.0
TINY = 1e-35
LANES = 128
SUBLANES = 8
UNROLL = 4
GRANT = pltpu.CompilerParams(vmem_limit_bytes=12 << 20)
VMEM = pl.BlockSpec(memory_space=pltpu.VMEM)
HBM = pl.BlockSpec(memory_space=pl.ANY)
SMEM = pl.BlockSpec(memory_space=pltpu.SMEM)


def tile(ref, row, group, col):
    return ref[row, pl.ds(group * SUBLANES, SUBLANES), pl.ds(col * LANES, LANES)]


def shifted(tiles, lane, shift):
    if shift == 0:
        return tiles
    zero = jnp.zeros_like(tiles[0])
    rolled = [pltpu.roll(t, (-shift) % LANES, 1) for t in tiles]
    if shift > 0:
        ahead = rolled[1:] + [zero]
        return [jnp.where(lane < LANES - shift, a, b) for a, b in zip(rolled, ahead)]
    behind = [zero] + rolled[:-1]
    return [jnp.where(lane >= -shift, a, b) for a, b in zip(rolled, behind)]


def blur_row(source, row, group, wx, wy, taps, reverse, lane, cols):
    radius = taps // 2
    planes = pl.ds(group * SUBLANES, SUBLANES)
    sums = None
    for tap in range(taps):
        at = row + (2 * radius - tap if reverse else tap)
        weight = wx[tap, planes, :]
        terms = [weight * tile(source, at, group, col) for col in range(cols)]
        sums = terms if sums is None else [a + b for a, b in zip(sums, terms)]
    result = None
    for tap in range(taps):
        weight = wy[tap, planes, :]
        moved = shifted(sums, lane, radius - tap if reverse else tap - radius)
        terms = [weight * m for m in moved]
        result = terms if result is None else [a + b for a, b in zip(result, terms)]
    return result


def near_core(*values):
    return [pltpu.with_memory_space_constraint(value, pltpu.VMEM) for value in values]


def far_memory(*values):
    return [pltpu.with_memory_space_constraint(value, pltpu.HBM) for value in values]


def position(cores):
    brick = lax.axis_index("brick")
    return lax.div(brick, cores), lax.rem(brick, cores), lax.axis_index("view")


def ratio_range(bricks, taps):
    least = CAMERA[0] / (taps * taps * PSF[1] * PSF[1] * ESTIMATE[1])
    inside = taps // 2 + 1
    most = bricks * CAMERA[1] / (inside * inside * PSF[0] * PSF[0] * ESTIMATE[0])
    low, high = math.log(least) - 0.01, math.log(most) + 0.01
    return low, (high - low) / (2 * CODE_TOP - 1)


def encode_ratio(value, bricks, taps):
    low, step = ratio_range(bricks, taps)
    tiny = math.exp(low)
    code = jnp.round((jnp.log(jnp.maximum(value, tiny)) - low) * (1.0 / step)) + (1.0 - CODE_TOP)
    code = jnp.where(value > 0, jnp.minimum(code, CODE_TOP), -CODE_TOP)
    return code.astype(jnp.int32).astype(jnp.int16)


def decode_ratio(code, bricks, taps):
    low, step = ratio_range(bricks, taps)
    code = code.astype(jnp.int32).astype(jnp.float32)
    value = jnp.exp((code + (CODE_TOP - 1.0)) * step + low)
    return jnp.where(code > -CODE_TOP, value, 0.0)


def encode_estimate(value):
    scale = 2 * CODE_TOP / (ESTIMATE[1] - ESTIMATE[0])
    code = jnp.round((value - ESTIMATE[0]) * scale) - CODE_TOP
    return code.astype(jnp.int32).astype(jnp.int16)


def decode_estimate(code):
    scale = (ESTIMATE[1] - ESTIMATE[0]) / (2 * CODE_TOP)
    return (code.astype(jnp.int32).astype(jnp.float32) + CODE_TOP) * scale + ESTIMATE[0]


def encode_rows(value):
    most = jnp.maximum(jnp.max(value, axis=-1, keepdims=True), TINY)
    level = jnp.ceil(jnp.log(most) * (SCALE_STEPS / math.log(2.0))) + 1.0
    factor = jnp.exp(level * (-math.log(2.0) / SCALE_STEPS)) * (2 * CODE_TOP)
    code = jnp.minimum(jnp.round(value * factor), 2 * CODE_TOP) - CODE_TOP
    return code.astype(jnp.int32).astype(jnp.int16), level


def decode_row(code, levels, row):
    levels = levels[:, row : row + 1].astype(jnp.int32).astype(jnp.float32)
    factor = jnp.exp(levels * (math.log(2.0) / SCALE_STEPS)) * (1.0 / (2 * CODE_TOP))
    return (code.astype(jnp.int32).astype(jnp.float32) + CODE_TOP) * factor


def pack_body(listed, blocks, estimate, out, edges, mine, theirs, held, lists, sems):
    chips, cores, views, slots, _, width = out.shape
    here = lax.axis_index("brick")
    _, core, view = position(cores)
    part = mine.shape[1]
    copies = [
        pltpu.make_async_copy(blocks, held, sems.at[0]),
        pltpu.make_async_copy(listed, lists, sems.at[3]),
    ]
    for index, (half, target) in enumerate(((core, mine), (1 - core, theirs))):
        begin = pl.multiple_of((view * cores + half) * part, part)
        copies.append(pltpu.make_async_copy(
            estimate.at[:, pl.ds(begin, part), :], target, sems.at[1 + index]))
    for copy in reversed(copies):
        copy.start()
    copies[2].wait()
    edges[core] = encode_estimate(mine[...])
    copies[3].wait()
    edges[1 - core] = encode_estimate(theirs[...])
    copies[1].wait()
    copies[0].wait()

    def one_chip(chip, carry):
        for slot in range(slots):
            block = jnp.maximum(lists[cores * chip + cores - 1, slot, here], 0)
            for half in range(cores):
                for other in range(views):
                    begin = (other * cores + half) * width
                    out[chip, half, other, slot] = held[block, :, begin : begin + width]
        return carry

    lax.fori_loop(0, chips, one_chip, 0, unroll=2)


def blur_body(layout, table, mine, partner, across, passed, inverse, wx, wy, field):
    views, part, cores, taps, kernels = (
        layout["views"], layout["part"], layout["cores"], layout["taps"], layout["kernels"])
    chip, core, view_here = position(cores)
    where = view_here * cores + core
    has_top = (chip > 0).astype(jnp.float32)
    has_bottom = (chip < layout["bricks"] // cores - 1).astype(jnp.float32)
    first = core == 0
    radius = taps // 2
    direct = decode_estimate(across[core])
    relayed = decode_estimate(passed[...])
    rows = (jnp.where(first, direct, relayed)[mine.shape[0] - radius :] * has_top,
            jnp.where(first, mine[...], partner[...]), jnp.where(first, partner[...], mine[...]),
            jnp.where(first, relayed, direct)[: 2 * radius] * has_bottom)
    for view in range(views):
        base = view * layout["table"]

        def one_plane(plane, carry):
            pick = table[base + layout["index_at"] + where * part + plane].astype(jnp.int32)
            for axis, target in enumerate((wx, wy)):
                begin = base + layout["bank_at"] + (axis * kernels + pick) * taps
                for tap in range(taps):
                    target[tap, pl.ds(view * part + plane, 1), :] = jnp.full(
                        (1, LANES), table[begin + tap], jnp.float32)
            return carry

        lax.fori_loop(0, part, one_plane, 0)
        planes = slice(view * part, (view + 1) * part)
        at = 0
        for piece in rows:
            field[at : at + piece.shape[0], planes, :] = piece
            at += piece.shape[0]
    rows_out, planes, columns = inverse.shape
    own_rows = cores * layout["rows_dev"]
    lane = lax.broadcasted_iota(jnp.int32, (SUBLANES, LANES), 1)

    def one_row(row, carry):
        wanted = jnp.where(row < own_rows, 1.0, has_bottom)
        for group in range(planes // SUBLANES):
            tiles = blur_row(field, row, group, wx, wy, taps, False, lane, columns // LANES)
            for col, value in enumerate(tiles):
                inverse[row, pl.ds(group * SUBLANES, SUBLANES), pl.ds(col * LANES, LANES)] = wanted / value
        return carry

    lax.fori_loop(0, rows_out, one_row, 0, unroll=2)


def ratio_row(layout, placed, inverse, field, turned, row):
    _, planes, columns = field.shape
    radius = layout["taps"] // 2
    block_width, pitch = layout["block_width"], layout["pitch"]
    per_tile = LANES // block_width
    groups = planes // per_tile
    lane = lax.broadcasted_iota(jnp.int32, (groups, LANES), 1)
    for col in range(columns // LANES):
        tiles = [
            placed[pl.ds((col * per_tile + k) * groups * pitch + row, groups, stride=pitch), :]
            for k in range(per_tile)
        ]
        step = per_tile // 2
        while step:
            width = step * block_width
            first_half = (lane // width) % 2 == 0
            mixed = list(tiles)
            for k in range(per_tile):
                if (k // step) % 2 == 0:
                    a, b = tiles[k], tiles[k + step]
                    mixed[k] = jnp.where(first_half, a, pltpu.roll(b, width, 1))
                    mixed[k + step] = jnp.where(first_half, pltpu.roll(a, LANES - width, 1), b)
            tiles = mixed
            step //= 2
        for k, value in enumerate(tiles):
            turned[pl.ds(col * planes + k, groups, stride=per_tile), :] = value
    for col in range(columns // LANES):
        for group in range(planes // SUBLANES):
            measured = turned[pl.ds(col * planes + group * SUBLANES, SUBLANES), :]
            planes_at = pl.ds(group * SUBLANES, SUBLANES)
            field[row + radius, planes_at, pl.ds(col * LANES, LANES)] = (
                measured * tile(inverse, row, group, col))


def ratio_body(layout, table, arrived, inverse, placed, field, upward, downward, turned):
    views, cores, slots, taps = layout["views"], layout["cores"], layout["slots"], layout["taps"]
    bricks, per_holder, rows_dev = layout["bricks"], layout["per_holder"], layout["rows_dev"]
    radius = taps // 2
    per_tile = LANES // layout["block_width"]
    depth_tiles = layout["part"] // per_tile
    groups = views * depth_tiles
    pitch = layout["pitch"]
    chip, _, _ = position(cores)
    first_row = chip * cores * rows_dev
    placed[...] = jnp.zeros_like(placed)

    def one_source(source, carry):
        adds = []
        for view in range(views):
            base = view * layout["table"]
            for slot in range(slots):
                listed = table[base + slot * bricks + source].astype(jnp.int32)
                named = listed >= 0
                block = jnp.maximum(listed, 0)
                start = table[base + layout["offset_at"] + source * per_holder + block]
                start = jnp.where(named, start.astype(jnp.int32) - first_row, 0)
                target = jnp.where(named, block, per_holder)
                values = arrived[source * views + view, slot].astype(jnp.float32)
                for z_tile in range(depth_tiles):
                    begin = (target * groups + view * depth_tiles + z_tile) * pitch + start
                    adds.append((begin, values[:, z_tile * LANES : (z_tile + 1) * LANES]))
        held = [placed[pl.ds(begin, rows_dev), :] for begin, _ in adds]
        for (begin, value), old in zip(adds, held):
            placed[pl.ds(begin, rows_dev), :] = old + value
        return carry

    lax.fori_loop(0, bricks, one_source, 0, unroll=UNROLL)

    own_rows = cores * rows_dev
    for target, begin in ((upward, own_rows - radius), (downward, 0)):

        def one_row(row, carry):
            ratio_row(layout, placed, inverse, field, turned, row + begin)
            target[row] = encode_ratio(field[row + begin + radius], bricks, taps)
            return carry

        lax.fori_loop(0, target.shape[0], one_row, 0, unroll=2)


def own_body(layout, placed, inverse, edges, wx, wy, field, done, turned):
    rows, planes, columns = done.shape
    radius = layout["taps"] // 2
    lane = lax.broadcasted_iota(jnp.int32, (SUBLANES, LANES), 1)
    field[0:radius] = jnp.zeros((radius, planes, columns), jnp.float32)

    def inner_row(row, carry):
        ratio_row(layout, placed, inverse, field, turned, row)
        return carry

    lax.fori_loop(radius, rows - radius, inner_row, 0)

    def one_row(row, carry):
        for group in range(planes // SUBLANES):
            tiles = blur_row(field, row, group, wx, wy, layout["taps"], True, lane, columns // LANES)
            for col, value in enumerate(tiles):
                done[row, pl.ds(group * SUBLANES, SUBLANES), pl.ds(col * LANES, LANES)] = value
        return carry

    lax.fori_loop(0, rows, one_row, 0, unroll=2)


def rest_body(layout, flip, done, before, after, wx, wy, source, target, reach, total):
    views, part, cores, taps = layout["views"], layout["part"], layout["cores"], layout["taps"]
    bricks, rows_dev = layout["bricks"], layout["rows_dev"]
    _, planes, columns = done.shape
    radius = taps // 2
    chip, core, _ = position(cores)
    lane = lax.broadcasted_iota(jnp.int32, (SUBLANES, LANES), 1)
    cols = columns // LANES

    def add_received(half):
        message, there = (
            (after, chip < bricks // cores - 1) if half else (before, chip > 0))
        mask = there.astype(jnp.float32)

        def one_message_row(row, carry):
            reach[row] = decode_ratio(message[row], bricks, taps) * mask
            return carry

        lax.fori_loop(0, message.shape[0], one_message_row, 0, unroll=UNROLL)
        first = rows_dev if half else -radius

        def one_group(group, carry):
            planes_at = pl.ds(pl.multiple_of(group * SUBLANES, SUBLANES), SUBLANES)
            for row in range(rows_dev):
                result = [
                    done[half * rows_dev + row, planes_at, pl.ds(col * LANES, LANES)]
                    for col in range(cols)
                ]
                sums = None
                for tap in range(taps):
                    at = row + radius - tap - first
                    if not 0 <= at < message.shape[0]:
                        continue
                    weight = wx[tap, planes_at, :]
                    terms = [
                        weight * reach[at, planes_at, pl.ds(col * LANES, LANES)] for col in range(cols)]
                    sums = terms if sums is None else [a + b for a, b in zip(sums, terms)]
                for tap in range(taps if sums else 0):
                    weight = wy[tap, planes_at, :]
                    moved = shifted(sums, lane, radius - tap)
                    result = [a + weight * m for a, m in zip(result, moved)]
                for col, value in enumerate(result):
                    total[row, planes_at, pl.ds(col * LANES, LANES)] = value
            return carry

        lax.fori_loop(0, planes // SUBLANES, one_group, 0)

    this = 1 - core if flip else core
    for half in range(cores):
        pl.when(this == half)(functools.partial(add_received, half))
    wide = lax.broadcasted_iota(jnp.int32, (part, LANES), 1)
    levels = jnp.zeros((part, LANES), jnp.float32)
    for row in range(rows_dev):
        value = source[row]
        for view in range(views):
            value = value * total[row, view * part : (view + 1) * part, :]
        target[:, row * columns : (row + 1) * columns], level = encode_rows(value)
        levels = jnp.where(wide == row, level, levels)
    target[:, rows_dev * columns :] = levels.astype(jnp.int32).astype(jnp.int16)


def join_body(places, *refs):
    _, core, view = position(2)
    count = len(places)
    sources, (out, held, sems) = refs[:count], refs[-3:]
    rows, columns = out.shape[0], out.shape[2]
    part = sources[0].shape[0]
    copies = []
    for index, (piece, (turn, flip)) in enumerate(zip(sources, places)):
        v = 1 - view if turn else view
        c = 1 - core if flip else core
        levels = piece[:, rows * columns :]
        for row in range(rows):
            held[index, row] = decode_row(piece[:, row * columns : (row + 1) * columns], levels, row)
        begin = pl.multiple_of((v * 2 + c) * part, part)
        copies.append(pltpu.make_async_copy(
            held.at[index], out.at[:, pl.ds(begin, part), :], sems.at[index]))
        copies[-1].start()
    for copy in copies:
        copy.wait()


def join(shape, part, places, pieces, out=None):
    rows, _, columns = shape
    count = len(pieces)
    return pl.pallas_call(
        functools.partial(join_body, places),
        out_shape=jax.ShapeDtypeStruct(shape, jnp.float32),
        in_specs=[VMEM] * count + ([] if out is None else [HBM]),
        out_specs=HBM,
        input_output_aliases={} if out is None else {count: 0},
        scratch_shapes=[
            pltpu.VMEM((count, rows, part, columns), jnp.float32), pltpu.SemaphoreType.DMA((count,))],
        compiler_params=GRANT,
        name="join",
    )(*near_core(*pieces), *([] if out is None else [out]))


def shards(estimate, camera_blocks, block_lists, block_offsets, psf_index, psf_bank):
    rows_dev, depth, columns = estimate.shape
    _, per_holder, block_rows, block_lanes = camera_blocks.shape
    bricks, slots = block_lists.shape[1], block_lists.shape[3]
    views = lax.axis_size("view")
    kernels, taps = psf_bank.shape[2:]
    radius = taps // 2
    cores = 2
    chips = bricks // cores
    part = depth // (cores * views)
    planes = views * part
    block_width = block_lanes // depth
    brick = lax.axis_index("brick")
    view = lax.axis_index("view")
    core = lax.rem(brick, cores)
    f32 = jnp.float32

    lists = block_lists[0].transpose(0, 2, 1)
    outgoing = pltpu.VMEM(
        (chips, cores, views, slots, block_rows, part * block_width), camera_blocks.dtype)
    piece = pltpu.VMEM((rows_dev, part, columns), f32)
    coded = pltpu.VMEM((cores, rows_dev, part, columns), jnp.int16)
    packed, edges, mine, theirs = pl.pallas_call(
        pack_body,
        out_shape=[outgoing, coded, piece, piece],
        in_specs=[HBM] * 3,
        out_specs=[VMEM] * 4,
        scratch_shapes=[
            pltpu.VMEM(camera_blocks.shape[1:], camera_blocks.dtype),
            pltpu.SMEM(lists.shape, jnp.int32),
            pltpu.SemaphoreType.DMA((4,)),
        ],
        compiler_params=GRANT,
        name="pack",
    )(*far_memory(lists, camera_blocks[0], estimate))
    swap = [(i, i ^ 1) for i in range(bricks)]
    packed = packed.reshape(bricks * views, slots, block_rows, part * block_width)
    across = lax.ppermute(edges, "brick", [
        (i, j) for i in range(bricks) for j in [i + 1 if i % cores else i - 1]
        if 0 <= j < bricks])
    partner = lax.ppermute(theirs, "brick", swap)
    arrived = lax.all_to_all(packed, ("brick", "view"), 0, 0, tiled=True)

    route = lax.dynamic_index_in_dim(lists, brick - core + cores - 1, 0, keepdims=False)
    pieces = [route.reshape(-1), block_offsets[0], psf_index[0], psf_bank[0].reshape(-1)]
    starts = [0]
    for piece in pieces:
        starts.append(starts[-1] + piece.shape[0])
    length = -(-starts[-1] // LANES) * LANES
    table = jnp.concatenate(
        [piece.astype(f32) for piece in pieces] + [jnp.zeros((length - starts[-1],), f32)])
    if views == 2:
        other = lax.ppermute(table, "view", [(0, 1), (1, 0)])
    layout = dict(
        views=views, part=part, cores=cores, taps=taps, kernels=kernels, slots=slots, bricks=bricks,
        per_holder=per_holder, rows_dev=rows_dev, block_width=block_width, table=length,
        offset_at=starts[1], index_at=starts[2], bank_at=starts[3],
        pitch=cores * rows_dev + 2 * radius + 1)

    up = [(i, i + cores) for i in range(bricks - cores)]
    down = [(i + cores, i) for i in range(bricks - cores)]
    passed = lax.ppermute(
        lax.dynamic_index_in_dim(across, 1 - core, 0, keepdims=False), "brick", swap)
    if views == 2:
        table = jnp.concatenate(
            [jnp.where(view == 0, table, other), jnp.where(view == 0, other, table)])
    else:
        table = lax.all_gather(table, "view", tiled=True)

    own_rows = cores * rows_dev
    rows_all = own_rows + radius
    groups = planes * block_width // LANES
    placing = pltpu.VMEM(((per_holder + 1) * groups * layout["pitch"], LANES), f32)
    inverse, wx, wy = pl.pallas_call(
        functools.partial(blur_body, layout),
        out_shape=[
            pltpu.VMEM((rows_all, planes, columns), f32),
            pltpu.VMEM((taps, planes, LANES), f32),
            pltpu.VMEM((taps, planes, LANES), f32),
        ],
        in_specs=[SMEM] + [VMEM] * 4,
        out_specs=[VMEM] * 3,
        scratch_shapes=[pltpu.VMEM((rows_all + 2 * radius, planes, columns), f32)],
        compiler_params=GRANT,
        name="blur",
    )(table, *near_core(mine, partner, across, passed))

    edged = pltpu.VMEM((rows_all + radius, planes, columns), f32)
    turning = pltpu.VMEM((columns // LANES * planes, LANES), f32)
    placed, field, upward, downward = pl.pallas_call(
        functools.partial(ratio_body, layout),
        out_shape=[
            placing,
            edged,
            pltpu.VMEM((2 * radius, planes, columns), jnp.int16),
            pltpu.VMEM((radius, planes, columns), jnp.int16),
        ],
        in_specs=[SMEM] + [VMEM] * 2,
        out_specs=[VMEM] * 4,
        scratch_shapes=[turning],
        compiler_params=GRANT,
        name="ratio",
    )(table, *near_core(arrived, inverse))

    before = lax.ppermute(upward, "brick", up)
    after = lax.ppermute(downward, "brick", down)
    _, done = pl.pallas_call(
        functools.partial(own_body, layout),
        out_shape=[edged, pltpu.VMEM((own_rows, planes, columns), f32)],
        in_specs=[VMEM] * 5,
        out_specs=[VMEM] * 2,
        input_output_aliases={2: 0},
        scratch_shapes=[turning],
        compiler_params=GRANT,
        name="own",
    )(*near_core(placed, inverse, field, wx, wy))

    def finished(flip, source):
        return pl.pallas_call(
            functools.partial(rest_body, layout, flip),
            out_shape=pltpu.VMEM((part, rows_dev * columns + LANES), jnp.int16),
            in_specs=[VMEM] * 6,
            out_specs=VMEM,
            scratch_shapes=[
                pltpu.VMEM((2 * radius, planes, columns), f32),
                pltpu.VMEM((rows_dev, planes, columns), f32),
            ],
            compiler_params=GRANT,
            name="rest",
        )(*near_core(done, before, after, wx, wy), source)

    if views == 2:
        turn = [(0, 1), (1, 0)]
        keep = finished(False, mine)
        far = lax.ppermute(keep, "view", turn)
        send = finished(True, partner)
        far_near = lax.ppermute(send, ("brick", "view"), [
            (i * views + j, (i ^ 1) * views + 1 - j)
            for i in range(bricks) for j in range(views)])
        near = lax.ppermute(send, "brick", swap)
        out = join(estimate.shape, part, ((False, False), (False, True)), (keep, near))
        out = join(estimate.shape, part, ((True, False),), (far,), out)
        return join(estimate.shape, part, ((True, True),), (far_near,), out)
    keep = finished(False, mine)
    near = lax.ppermute(finished(True, partner), "brick", swap)
    both = jnp.stack([jnp.where(core == 0, keep, near), jnp.where(core == 0, near, keep)])
    coded = lax.all_gather(both, "view").reshape((-1,) + keep.shape)
    rows = [
        jax.vmap(lambda piece, row=row: decode_row(
            piece[:, row * columns : (row + 1) * columns], piece[:, rows_dev * columns :], row))(coded)
        for row in range(rows_dev)
    ]
    return jnp.stack(rows).reshape(estimate.shape)


def solution(mesh):
    placed = (
        P("brick", None, None),
        P("view", "brick", None, None),
        P("view", None, None, None),
        P("view", None),
        P("view", None),
        P("view", None, None, None),
    )
    return jax.shard_map(
        shards, mesh=mesh, in_specs=placed, out_specs=P("brick", None, None), check_vma=False
    )
```

```python
import functools
import math

import jax
import jax.numpy as jnp
from jax import lax
from jax.experimental import pallas as pl
from jax.experimental.pallas import tpu as pltpu
from jax.sharding import PartitionSpec as P


CAMERA = (0.099609375, 2.0)
PSF = (0.03, 0.3)
ESTIMATE = (0.5, 2.0)
CODE_TOP = 32767.0
SCALE_STEPS = 64.0
TINY = 1e-35
LANES = 128
SUBLANES = 8
UNROLL = 4
GRANT = pltpu.CompilerParams(vmem_limit_bytes=12 << 20)
VMEM = pl.BlockSpec(memory_space=pltpu.VMEM)
HBM = pl.BlockSpec(memory_space=pl.ANY)
SMEM = pl.BlockSpec(memory_space=pltpu.SMEM)


def tile(ref, row, group, col):
    return ref[row, pl.ds(group * SUBLANES, SUBLANES), pl.ds(col * LANES, LANES)]


def shifted(tiles, lane, shift):
    if shift == 0:
        return tiles
    zero = jnp.zeros_like(tiles[0])
    rolled = [pltpu.roll(t, (-shift) % LANES, 1) for t in tiles]
    if shift > 0:
        ahead = rolled[1:] + [zero]
        return [jnp.where(lane < LANES - shift, a, b) for a, b in zip(rolled, ahead)]
    behind = [zero] + rolled[:-1]
    return [jnp.where(lane >= -shift, a, b) for a, b in zip(rolled, behind)]


def blur_row(source, row, group, wx, wy, taps, reverse, lane, cols):
    radius = taps // 2
    planes = pl.ds(group * SUBLANES, SUBLANES)
    sums = None
    for tap in range(taps):
        at = row + (2 * radius - tap if reverse else tap)
        weight = wx[tap, planes, :]
        terms = [weight * tile(source, at, group, col) for col in range(cols)]
        sums = terms if sums is None else [a + b for a, b in zip(sums, terms)]
    result = None
    for tap in range(taps):
        weight = wy[tap, planes, :]
        moved = shifted(sums, lane, radius - tap if reverse else tap - radius)
        terms = [weight * m for m in moved]
        result = terms if result is None else [a + b for a, b in zip(result, terms)]
    return result


def near_core(*values):
    return [pltpu.with_memory_space_constraint(value, pltpu.VMEM) for value in values]


def far_memory(*values):
    return [pltpu.with_memory_space_constraint(value, pltpu.HBM) for value in values]


def position(cores):
    brick = lax.axis_index("brick")
    return lax.div(brick, cores), lax.rem(brick, cores), lax.axis_index("view")


def ratio_range(bricks, taps):
    least = CAMERA[0] / (taps * taps * PSF[1] * PSF[1] * ESTIMATE[1])
    inside = taps // 2 + 1
    most = bricks * CAMERA[1] / (inside * inside * PSF[0] * PSF[0] * ESTIMATE[0])
    low, high = math.log(least) - 0.01, math.log(most) + 0.01
    return low, (high - low) / (2 * CODE_TOP - 1)


def encode_ratio(value, bricks, taps):
    low, step = ratio_range(bricks, taps)
    tiny = math.exp(low)
    code = jnp.log(jnp.maximum(value, tiny)) * (1.0 / step) + (1.5 - low / step)
    code = jnp.where(value > 0, jnp.minimum(code, 2 * CODE_TOP), 0.0)
    return (code.astype(jnp.int32) - int(CODE_TOP)).astype(jnp.int16)


def decode_ratio(code, bricks, taps):
    low, step = ratio_range(bricks, taps)
    code = code.astype(jnp.int32).astype(jnp.float32)
    value = jnp.exp((code + (CODE_TOP - 1.0)) * step + low)
    return jnp.where(code > -CODE_TOP, value, 0.0)


def encode_estimate(value):
    scale = 2 * CODE_TOP / (ESTIMATE[1] - ESTIMATE[0])
    code = (value - ESTIMATE[0]) * scale + 0.5
    return (code.astype(jnp.int32) - int(CODE_TOP)).astype(jnp.int16)


def decode_estimate(code):
    scale = (ESTIMATE[1] - ESTIMATE[0]) / (2 * CODE_TOP)
    return (code.astype(jnp.int32).astype(jnp.float32) + CODE_TOP) * scale + ESTIMATE[0]


def encode_rows(value):
    most = jnp.maximum(jnp.max(value, axis=-1, keepdims=True), TINY)
    level = jnp.ceil(jnp.log(most) * (SCALE_STEPS / math.log(2.0))) + 1.0
    factor = jnp.exp(level * (-math.log(2.0) / SCALE_STEPS)) * (2 * CODE_TOP)
    code = jnp.minimum(value * factor + 0.5, 2 * CODE_TOP).astype(jnp.int32) - int(CODE_TOP)
    return code.astype(jnp.int16), level


def decode_row(code, levels, row):
    levels = levels[:, row : row + 1].astype(jnp.int32).astype(jnp.float32)
    factor = jnp.exp(levels * (math.log(2.0) / SCALE_STEPS)) * (1.0 / (2 * CODE_TOP))
    return (code.astype(jnp.int32).astype(jnp.float32) + CODE_TOP) * factor


def pack_body(listed, blocks, estimate, out, edges, mine, theirs, held, lists, sems):
    chips, cores, views, slots, _, width = out.shape
    here = lax.axis_index("brick")
    _, core, view = position(cores)
    part = mine.shape[1]
    copies = [
        pltpu.make_async_copy(blocks, held, sems.at[0]),
        pltpu.make_async_copy(listed, lists, sems.at[3]),
    ]
    for index, (half, target) in enumerate(((core, mine), (1 - core, theirs))):
        begin = pl.multiple_of((view * cores + half) * part, part)
        copies.append(pltpu.make_async_copy(
            estimate.at[:, pl.ds(begin, part), :], target, sems.at[1 + index]))
    for copy in reversed(copies):
        copy.start()
    copies[2].wait()
    edges[core] = encode_estimate(mine[...])
    copies[3].wait()
    edges[1 - core] = encode_estimate(theirs[...])
    copies[1].wait()
    copies[0].wait()

    def one_chip(chip, carry):
        for slot in range(slots):
            block = jnp.maximum(lists[cores * chip + cores - 1, slot, here], 0)
            for half in range(cores):
                for other in range(views):
                    begin = (other * cores + half) * width
                    out[chip, half, other, slot] = held[block, :, begin : begin + width]
        return carry

    lax.fori_loop(0, chips, one_chip, 0, unroll=2)


def place_blocks(layout, table, begins):
    views, cores, slots = layout["views"], layout["cores"], layout["slots"]
    bricks, per_holder, rows_dev = layout["bricks"], layout["per_holder"], layout["rows_dev"]
    depth_tiles = layout["part"] * layout["block_width"] // LANES
    chip, _, _ = position(cores)
    first_row = chip * cores * rows_dev

    def one_source(source, carry):
        for view in range(views):
            base = view * layout["table"]
            for slot in range(slots):
                listed = table[base + slot * bricks + source].astype(jnp.int32)
                named = listed >= 0
                block = jnp.maximum(listed, 0)
                start = table[base + layout["offset_at"] + source * per_holder + block]
                start = jnp.where(named, start.astype(jnp.int32) - first_row, 0)
                tile_at = jnp.where(named, block, per_holder) * views + view
                begins[(source * views + view) * slots + slot] = (
                    tile_at * depth_tiles * layout["pitch"] + start)
        return carry

    lax.fori_loop(0, bricks, one_source, 0)


def blur_body(layout, table, mine, partner, across, passed, inverse, wx, wy, begins, field):
    views, part, cores, taps, kernels = (
        layout["views"], layout["part"], layout["cores"], layout["taps"], layout["kernels"])
    chip, core, view_here = position(cores)
    where = view_here * cores + core
    has_top = (chip > 0).astype(jnp.float32)
    has_bottom = (chip < layout["bricks"] // cores - 1).astype(jnp.float32)
    first = core == 0
    radius = taps // 2
    direct = decode_estimate(across[core])
    relayed = decode_estimate(passed[...])
    rows = (jnp.where(first, direct, relayed)[mine.shape[0] - radius :] * has_top,
            jnp.where(first, mine[...], partner[...]), jnp.where(first, partner[...], mine[...]),
            jnp.where(first, relayed, direct)[: 2 * radius] * has_bottom)
    for view in range(views):
        base = view * layout["table"]

        def one_plane(plane, carry):
            pick = table[base + layout["index_at"] + where * part + plane].astype(jnp.int32)
            for axis, target in enumerate((wx, wy)):
                begin = base + layout["bank_at"] + (axis * kernels + pick) * taps
                for tap in range(taps):
                    target[tap, pl.ds(view * part + plane, 1), :] = jnp.full(
                        (1, LANES), table[begin + tap], jnp.float32)
            return carry

        lax.fori_loop(0, part, one_plane, 0)
        planes = slice(view * part, (view + 1) * part)
        at = 0
        for piece in rows:
            field[at : at + piece.shape[0], planes, :] = piece
            at += piece.shape[0]
    rows_out, planes, columns = inverse.shape
    own_rows = cores * layout["rows_dev"]
    lane = lax.broadcasted_iota(jnp.int32, (SUBLANES, LANES), 1)
    place_blocks(layout, table, begins)

    def one_row(row, carry):
        wanted = jnp.where(row < own_rows, 1.0, has_bottom)
        for group in range(planes // SUBLANES):
            tiles = blur_row(field, row, group, wx, wy, taps, False, lane, columns // LANES)
            for col, value in enumerate(tiles):
                inverse[row, pl.ds(group * SUBLANES, SUBLANES), pl.ds(col * LANES, LANES)] = wanted / value
        return carry

    lax.fori_loop(0, rows_out, one_row, 0, unroll=2)


def ratio_row(layout, placed, inverse, field, turned, row):
    _, planes, columns = field.shape
    radius = layout["taps"] // 2
    block_width, pitch = layout["block_width"], layout["pitch"]
    per_tile = LANES // block_width
    groups = planes // per_tile
    lane = lax.broadcasted_iota(jnp.int32, (groups, LANES), 1)
    for col in range(columns // LANES):
        tiles = [
            placed[pl.ds((col * per_tile + k) * groups * pitch + row, groups, stride=pitch), :]
            for k in range(per_tile)
        ]
        step = per_tile // 2
        while step:
            width = step * block_width
            first_half = (lane // width) % 2 == 0
            mixed = list(tiles)
            for k in range(per_tile):
                if (k // step) % 2 == 0:
                    a, b = tiles[k], tiles[k + step]
                    mixed[k] = jnp.where(first_half, a, pltpu.roll(b, width, 1))
                    mixed[k + step] = jnp.where(first_half, pltpu.roll(a, LANES - width, 1), b)
            tiles = mixed
            step //= 2
        for k, value in enumerate(tiles):
            turned[pl.ds(col * planes + k, groups, stride=per_tile), :] = value
    for col in range(columns // LANES):
        for group in range(planes // SUBLANES):
            measured = turned[pl.ds(col * planes + group * SUBLANES, SUBLANES), :]
            planes_at = pl.ds(group * SUBLANES, SUBLANES)
            field[row + radius, planes_at, pl.ds(col * LANES, LANES)] = (
                measured * tile(inverse, row, group, col))


def ratio_body(layout, begins, arrived, inverse, placed, field, upward, downward, turned):
    views, cores, slots, taps = layout["views"], layout["cores"], layout["slots"], layout["taps"]
    bricks, rows_dev = layout["bricks"], layout["rows_dev"]
    radius = taps // 2
    per_tile = LANES // layout["block_width"]
    depth_tiles = layout["part"] // per_tile
    pitch = layout["pitch"]
    placed[...] = jnp.zeros_like(placed)

    def one_source(source, carry):
        adds = []
        for view in range(views):
            for slot in range(slots):
                begin = begins[(source * views + view) * slots + slot]
                values = arrived[source * views + view, slot].astype(jnp.float32)
                for z_tile in range(depth_tiles):
                    adds.append((
                        begin + z_tile * pitch,
                        values[:, z_tile * LANES : (z_tile + 1) * LANES]))
        held = [placed[pl.ds(begin, rows_dev), :] for begin, _ in adds]
        for (begin, value), old in zip(adds, held):
            placed[pl.ds(begin, rows_dev), :] = old + value
        return carry

    lax.fori_loop(0, bricks, one_source, 0, unroll=UNROLL)
    own_rows = cores * rows_dev
    for target, begin in ((upward, own_rows - radius), (downward, 0)):

        def one_row(row, carry):
            ratio_row(layout, placed, inverse, field, turned, row + begin)
            target[row] = encode_ratio(field[row + begin + radius], bricks, taps)
            return carry

        lax.fori_loop(0, target.shape[0], one_row, 0, unroll=UNROLL)


def own_body(layout, placed, inverse, edges, wx, wy, field, done, turned):
    rows, planes, columns = done.shape
    radius = layout["taps"] // 2
    lane = lax.broadcasted_iota(jnp.int32, (SUBLANES, LANES), 1)
    field[0:radius] = jnp.zeros((radius, planes, columns), jnp.float32)

    def inner_row(row, carry):
        ratio_row(layout, placed, inverse, field, turned, row)
        return carry

    lax.fori_loop(radius, rows - radius, inner_row, 0)

    def one_row(row, carry):
        for group in range(planes // SUBLANES):
            tiles = blur_row(field, row, group, wx, wy, layout["taps"], True, lane, columns // LANES)
            for col, value in enumerate(tiles):
                done[row, pl.ds(group * SUBLANES, SUBLANES), pl.ds(col * LANES, LANES)] = value
        return carry

    lax.fori_loop(0, rows, one_row, 0, unroll=2)


def rest_body(layout, flip, done, before, after, wx, wy, source, target, reach, total):
    views, part, cores, taps = layout["views"], layout["part"], layout["cores"], layout["taps"]
    bricks, rows_dev = layout["bricks"], layout["rows_dev"]
    _, planes, columns = done.shape
    radius = taps // 2
    chip, core, _ = position(cores)
    lane = lax.broadcasted_iota(jnp.int32, (SUBLANES, LANES), 1)
    cols = columns // LANES

    def add_received(half):
        message, there = (
            (after, chip < bricks // cores - 1) if half else (before, chip > 0))
        mask = there.astype(jnp.float32)

        def one_message_row(row, carry):
            reach[row] = decode_ratio(message[row], bricks, taps) * mask
            return carry

        lax.fori_loop(0, message.shape[0], one_message_row, 0, unroll=UNROLL)
        first = rows_dev if half else -radius

        def one_group(group, carry):
            planes_at = pl.ds(pl.multiple_of(group * SUBLANES, SUBLANES), SUBLANES)
            for row in range(rows_dev):
                result = [
                    done[half * rows_dev + row, planes_at, pl.ds(col * LANES, LANES)]
                    for col in range(cols)
                ]
                sums = None
                for tap in range(taps):
                    at = row + radius - tap - first
                    if not 0 <= at < message.shape[0]:
                        continue
                    weight = wx[tap, planes_at, :]
                    terms = [
                        weight * reach[at, planes_at, pl.ds(col * LANES, LANES)] for col in range(cols)]
                    sums = terms if sums is None else [a + b for a, b in zip(sums, terms)]
                for tap in range(taps if sums else 0):
                    weight = wy[tap, planes_at, :]
                    moved = shifted(sums, lane, radius - tap)
                    result = [a + weight * m for a, m in zip(result, moved)]
                for col, value in enumerate(result):
                    total[row, planes_at, pl.ds(col * LANES, LANES)] = value
            return carry

        lax.fori_loop(0, planes // SUBLANES, one_group, 0)

    this = 1 - core if flip else core
    for half in range(cores):
        pl.when(this == half)(functools.partial(add_received, half))
    wide = lax.broadcasted_iota(jnp.int32, (part, LANES), 1)
    levels = jnp.zeros((part, LANES), jnp.float32)
    for row in range(rows_dev):
        value = source[row]
        for view in range(views):
            value = value * total[row, view * part : (view + 1) * part, :]
        target[:, row * columns : (row + 1) * columns], level = encode_rows(value)
        levels = jnp.where(wide == row, level, levels)
    target[:, rows_dev * columns :] = levels.astype(jnp.int32).astype(jnp.int16)


def join_body(places, *refs):
    _, core, view = position(2)
    count = len(places)
    sources, (out, held, sems) = refs[:count], refs[-3:]
    rows, columns = out.shape[0], out.shape[2]
    part = sources[0].shape[0]
    copies = []
    for index, (piece, (turn, flip)) in enumerate(zip(sources, places)):
        v = 1 - view if turn else view
        c = 1 - core if flip else core
        levels = piece[:, rows * columns :]
        for row in range(rows):
            held[index, row] = decode_row(piece[:, row * columns : (row + 1) * columns], levels, row)
        begin = pl.multiple_of((v * 2 + c) * part, part)
        copies.append(pltpu.make_async_copy(
            held.at[index], out.at[:, pl.ds(begin, part), :], sems.at[index]))
        copies[-1].start()
    for copy in copies:
        copy.wait()


def join(shape, part, places, pieces, out=None):
    rows, _, columns = shape
    count = len(pieces)
    return pl.pallas_call(
        functools.partial(join_body, places),
        out_shape=jax.ShapeDtypeStruct(shape, jnp.float32),
        in_specs=[VMEM] * count + ([] if out is None else [HBM]),
        out_specs=HBM,
        input_output_aliases={} if out is None else {count: 0},
        scratch_shapes=[
            pltpu.VMEM((count, rows, part, columns), jnp.float32), pltpu.SemaphoreType.DMA((count,))],
        compiler_params=GRANT,
        name="join",
    )(*near_core(*pieces), *([] if out is None else [out]))


def shards(estimate, camera_blocks, block_lists, block_offsets, psf_index, psf_bank):
    rows_dev, depth, columns = estimate.shape
    _, per_holder, block_rows, block_lanes = camera_blocks.shape
    bricks, slots = block_lists.shape[1], block_lists.shape[3]
    views = lax.axis_size("view")
    kernels, taps = psf_bank.shape[2:]
    radius = taps // 2
    cores = 2
    chips = bricks // cores
    part = depth // (cores * views)
    planes = views * part
    block_width = block_lanes // depth
    brick = lax.axis_index("brick")
    view = lax.axis_index("view")
    core = lax.rem(brick, cores)
    f32 = jnp.float32

    lists = block_lists[0].transpose(0, 2, 1)
    outgoing = pltpu.VMEM(
        (chips, cores, views, slots, block_rows, part * block_width), camera_blocks.dtype)
    piece = pltpu.VMEM((rows_dev, part, columns), f32)
    coded = pltpu.VMEM((cores, rows_dev, part, columns), jnp.int16)
    packed, edges, mine, theirs = pl.pallas_call(
        pack_body,
        out_shape=[outgoing, coded, piece, piece],
        in_specs=[HBM] * 3,
        out_specs=[VMEM] * 4,
        scratch_shapes=[
            pltpu.VMEM(camera_blocks.shape[1:], camera_blocks.dtype),
            pltpu.SMEM(lists.shape, jnp.int32),
            pltpu.SemaphoreType.DMA((4,)),
        ],
        compiler_params=GRANT,
        name="pack",
    )(*far_memory(lists, camera_blocks[0], estimate))
    swap = [(i, i ^ 1) for i in range(bricks)]
    packed = packed.reshape(bricks * views, slots, block_rows, part * block_width)
    across = lax.ppermute(edges, "brick", [
        (i, j) for i in range(bricks) for j in [i + 1 if i % cores else i - 1]
        if 0 <= j < bricks])
    partner = lax.ppermute(theirs, "brick", swap)
    arrived = lax.all_to_all(packed, ("brick", "view"), 0, 0, tiled=True)

    route = lax.dynamic_index_in_dim(lists, brick - core + cores - 1, 0, keepdims=False)
    pieces = [route.reshape(-1), block_offsets[0], psf_index[0], psf_bank[0].reshape(-1)]
    starts = [0]
    for piece in pieces:
        starts.append(starts[-1] + piece.shape[0])
    length = -(-starts[-1] // LANES) * LANES
    table = jnp.concatenate(
        [piece.astype(f32) for piece in pieces] + [jnp.zeros((length - starts[-1],), f32)])
    if views == 2:
        other = lax.ppermute(table, "view", [(0, 1), (1, 0)])
    layout = dict(
        views=views, part=part, cores=cores, taps=taps, kernels=kernels, slots=slots, bricks=bricks,
        per_holder=per_holder, rows_dev=rows_dev, block_width=block_width, table=length,
        offset_at=starts[1], index_at=starts[2], bank_at=starts[3],
        pitch=cores * rows_dev + radius + 1)

    up = [(i, i + cores) for i in range(bricks - cores)]
    down = [(i + cores, i) for i in range(bricks - cores)]
    passed = lax.ppermute(
        lax.dynamic_index_in_dim(across, 1 - core, 0, keepdims=False), "brick", swap)
    if views == 2:
        table = jnp.concatenate(
            [jnp.where(view == 0, table, other), jnp.where(view == 0, other, table)])
    else:
        table = lax.all_gather(table, "view", tiled=True)

    own_rows = cores * rows_dev
    rows_all = own_rows + radius
    groups = planes * block_width // LANES
    placing = pltpu.VMEM(((per_holder + 1) * groups * layout["pitch"], LANES), f32)
    inverse, wx, wy, begins = pl.pallas_call(
        functools.partial(blur_body, layout),
        out_shape=[
            pltpu.VMEM((rows_all, planes, columns), f32),
            pltpu.VMEM((taps, planes, LANES), f32),
            pltpu.VMEM((taps, planes, LANES), f32),
            pltpu.SMEM((bricks * views * slots,), jnp.int32),
        ],
        in_specs=[SMEM] + [VMEM] * 4,
        out_specs=[VMEM] * 3 + [SMEM],
        scratch_shapes=[pltpu.VMEM((rows_all + 2 * radius, planes, columns), f32)],
        compiler_params=GRANT,
        name="blur",
    )(table, *near_core(mine, partner, across, passed))

    edged = pltpu.VMEM((rows_all + radius, planes, columns), f32)
    turning = pltpu.VMEM((columns // LANES * planes, LANES), f32)
    placed, field, upward, downward = pl.pallas_call(
        functools.partial(ratio_body, layout),
        out_shape=[
            placing,
            edged,
            pltpu.VMEM((2 * radius, planes, columns), jnp.int16),
            pltpu.VMEM((radius, planes, columns), jnp.int16),
        ],
        in_specs=[SMEM] + [VMEM] * 2,
        out_specs=[VMEM] * 4,
        scratch_shapes=[turning],
        compiler_params=GRANT,
        name="ratio",
    )(pltpu.with_memory_space_constraint(begins, pltpu.SMEM), *near_core(arrived, inverse))

    before = lax.ppermute(upward, "brick", up)
    after = lax.ppermute(downward, "brick", down)
    _, done = pl.pallas_call(
        functools.partial(own_body, layout),
        out_shape=[edged, pltpu.VMEM((own_rows, planes, columns), f32)],
        in_specs=[VMEM] * 5,
        out_specs=[VMEM] * 2,
        input_output_aliases={2: 0},
        scratch_shapes=[turning],
        compiler_params=GRANT,
        name="own",
    )(*near_core(placed, inverse, field, wx, wy))

    def finished(flip, source):
        return pl.pallas_call(
            functools.partial(rest_body, layout, flip),
            out_shape=pltpu.VMEM((part, rows_dev * columns + LANES), jnp.int16),
            in_specs=[VMEM] * 6,
            out_specs=VMEM,
            scratch_shapes=[
                pltpu.VMEM((2 * radius, planes, columns), f32),
                pltpu.VMEM((rows_dev, planes, columns), f32),
            ],
            compiler_params=GRANT,
            name="rest",
        )(*near_core(done, before, after, wx, wy), source)

    if views == 2:
        turn = [(0, 1), (1, 0)]
        keep = finished(False, mine)
        far = lax.ppermute(keep, "view", turn)
        send = finished(True, partner)
        far_near = lax.ppermute(send, ("brick", "view"), [
            (i * views + j, (i ^ 1) * views + 1 - j)
            for i in range(bricks) for j in range(views)])
        near = lax.ppermute(send, "brick", swap)
        out = join(estimate.shape, part, ((False, False), (False, True)), (keep, near))
        out = join(estimate.shape, part, ((True, False),), (far,), out)
        return join(estimate.shape, part, ((True, True),), (far_near,), out)
    keep = finished(False, mine)
    near = lax.ppermute(finished(True, partner), "brick", swap)
    both = jnp.stack([jnp.where(core == 0, keep, near), jnp.where(core == 0, near, keep)])
    coded = lax.all_gather(both, "view").reshape((-1,) + keep.shape)
    rows = [
        jax.vmap(lambda piece, row=row: decode_row(
            piece[:, row * columns : (row + 1) * columns], piece[:, rows_dev * columns :], row))(coded)
        for row in range(rows_dev)
    ]
    return jnp.stack(rows).reshape(estimate.shape)


def solution(mesh):
    placed = (
        P("brick", None, None),
        P("view", "brick", None, None),
        P("view", None, None, None),
        P("view", None),
        P("view", None),
        P("view", None, None, None),
    )
    return jax.shard_map(
        shards, mesh=mesh, in_specs=placed, out_specs=P("brick", None, None), check_vma=False
    )
```

```python
import functools
import math

import jax
import jax.numpy as jnp
from jax import lax
from jax.experimental import pallas as pl
from jax.experimental.pallas import tpu as pltpu
from jax.sharding import PartitionSpec as P


CAMERA = (0.099609375, 2.0)
PSF = (0.03, 0.3)
ESTIMATE = (0.5, 2.0)
CODE_TOP = 32767.0
SCALE_STEPS = 64.0
TINY = 1e-35
LANES = 128
SUBLANES = 8
UNROLL = 4
GRANT = pltpu.CompilerParams(vmem_limit_bytes=12 << 20)
VMEM = pl.BlockSpec(memory_space=pltpu.VMEM)
HBM = pl.BlockSpec(memory_space=pl.ANY)
SMEM = pl.BlockSpec(memory_space=pltpu.SMEM)


def tile(ref, row, group, col):
    return ref[row, pl.ds(group * SUBLANES, SUBLANES), pl.ds(col * LANES, LANES)]


def shifted(tiles, lane, shift):
    if shift == 0:
        return tiles
    zero = jnp.zeros_like(tiles[0])
    rolled = [pltpu.roll(t, (-shift) % LANES, 1) for t in tiles]
    if shift > 0:
        ahead = rolled[1:] + [zero]
        return [jnp.where(lane < LANES - shift, a, b) for a, b in zip(rolled, ahead)]
    behind = [zero] + rolled[:-1]
    return [jnp.where(lane >= -shift, a, b) for a, b in zip(rolled, behind)]


def blur_row(source, row, group, wx, wy, taps, reverse, lane, cols):
    radius = taps // 2
    planes = pl.ds(group * SUBLANES, SUBLANES)
    sums = None
    for tap in range(taps):
        at = row + (2 * radius - tap if reverse else tap)
        weight = wx[tap, planes, :]
        terms = [weight * tile(source, at, group, col) for col in range(cols)]
        sums = terms if sums is None else [a + b for a, b in zip(sums, terms)]
    result = None
    for tap in range(taps):
        weight = wy[tap, planes, :]
        moved = shifted(sums, lane, radius - tap if reverse else tap - radius)
        terms = [weight * m for m in moved]
        result = terms if result is None else [a + b for a, b in zip(result, terms)]
    return result


def near_core(*values):
    return [pltpu.with_memory_space_constraint(value, pltpu.VMEM) for value in values]


def far_memory(*values):
    return [pltpu.with_memory_space_constraint(value, pltpu.HBM) for value in values]


def position(cores):
    brick = lax.axis_index("brick")
    return lax.div(brick, cores), lax.rem(brick, cores), lax.axis_index("view")


def ratio_range(bricks, taps):
    least = CAMERA[0] / (taps * taps * PSF[1] * PSF[1] * ESTIMATE[1])
    inside = taps // 2 + 1
    most = bricks * CAMERA[1] / (inside * inside * PSF[0] * PSF[0] * ESTIMATE[0])
    low, high = math.log(least) - 0.01, math.log(most) + 0.01
    return low, (high - low) / (2 * CODE_TOP - 1)


def encode_ratio(value, bricks, taps):
    low, step = ratio_range(bricks, taps)
    tiny = math.exp(low)
    code = jnp.log(jnp.maximum(value, tiny)) * (1.0 / step) + (1.5 - low / step)
    code = jnp.where(value > 0, jnp.minimum(code, 2 * CODE_TOP), 0.0)
    return (code.astype(jnp.int32) - int(CODE_TOP)).astype(jnp.int16)


def decode_ratio(code, bricks, taps):
    low, step = ratio_range(bricks, taps)
    code = code.astype(jnp.int32).astype(jnp.float32)
    value = jnp.exp((code + (CODE_TOP - 1.0)) * step + low)
    return jnp.where(code > -CODE_TOP, value, 0.0)


def encode_estimate(value):
    scale = 2 * CODE_TOP / (ESTIMATE[1] - ESTIMATE[0])
    code = (value - ESTIMATE[0]) * scale + 0.5
    return (code.astype(jnp.int32) - int(CODE_TOP)).astype(jnp.int16)


def decode_estimate(code):
    scale = (ESTIMATE[1] - ESTIMATE[0]) / (2 * CODE_TOP)
    return (code.astype(jnp.int32).astype(jnp.float32) + CODE_TOP) * scale + ESTIMATE[0]


def encode_rows(value):
    most = jnp.maximum(jnp.max(value, axis=-1, keepdims=True), TINY)
    level = jnp.ceil(jnp.log(most) * (SCALE_STEPS / math.log(2.0))) + 1.0
    factor = jnp.exp(level * (-math.log(2.0) / SCALE_STEPS)) * (2 * CODE_TOP)
    code = jnp.minimum(value * factor + 0.5, 2 * CODE_TOP).astype(jnp.int32) - int(CODE_TOP)
    return code.astype(jnp.int16), level


def decode_row(code, levels, row):
    levels = levels[:, row : row + 1].astype(jnp.int32).astype(jnp.float32)
    factor = jnp.exp(levels * (math.log(2.0) / SCALE_STEPS)) * (1.0 / (2 * CODE_TOP))
    return (code.astype(jnp.int32).astype(jnp.float32) + CODE_TOP) * factor


def pack_body(listed, blocks, estimate, out, edges, mine, theirs, held, staged, lists, sems):
    chips, cores, views, slots, _, width = out.shape
    here = lax.axis_index("brick")
    _, core, view = position(cores)
    part = mine.shape[1]
    copies = [
        pltpu.make_async_copy(blocks, held, sems.at[0]),
        pltpu.make_async_copy(listed, lists, sems.at[3]),
    ]
    for index, (half, target) in enumerate(((core, mine), (1 - core, theirs))):
        begin = pl.multiple_of((view * cores + half) * part, part)
        copies.append(pltpu.make_async_copy(
            estimate.at[:, pl.ds(begin, part), :], target, sems.at[1 + index]))
    for index in (1, 0, 2, 3):
        copies[index].start()
    copies[1].wait()
    copies[0].wait()

    def one_chip(chip, carry):
        for slot in range(slots):
            block = jnp.maximum(lists[cores * chip + cores - 1, slot, here], 0)
            for half in range(cores):
                for other in range(views):
                    begin = (other * cores + half) * width
                    staged[chip, half, other, slot] = held[block, :, begin : begin + width]
        return carry

    lax.fori_loop(0, chips, one_chip, 0, unroll=2)
    leaving = pltpu.make_async_copy(staged, out, sems.at[4])
    leaving.start()
    copies[2].wait()
    edges[core] = encode_estimate(mine[...])
    copies[3].wait()
    edges[1 - core] = encode_estimate(theirs[...])
    leaving.wait()


def clear_body(earlier, out):
    out[...] = jnp.zeros_like(out)


def place_blocks(layout, table, begins):
    views, cores, slots = layout["views"], layout["cores"], layout["slots"]
    bricks, per_holder, rows_dev = layout["bricks"], layout["per_holder"], layout["rows_dev"]
    depth_tiles = layout["part"] * layout["block_width"] // LANES
    chip, _, _ = position(cores)
    first_row = chip * cores * rows_dev

    def one_source(source, carry):
        for view in range(views):
            base = view * layout["table"]
            for slot in range(slots):
                listed = table[base + slot * bricks + source].astype(jnp.int32)
                named = listed >= 0
                block = jnp.maximum(listed, 0)
                start = table[base + layout["offset_at"] + source * per_holder + block]
                start = jnp.where(named, start.astype(jnp.int32) - first_row, 0)
                tile_at = jnp.where(named, block, per_holder) * views + view
                begins[(source * views + view) * slots + slot] = (
                    tile_at * depth_tiles * layout["pitch"] + start)
        return carry

    lax.fori_loop(0, bricks, one_source, 0)


def blur_body(layout, table, mine, partner, across, passed, inverse, wx, wy, begins, field):
    views, part, cores, taps, kernels = (
        layout["views"], layout["part"], layout["cores"], layout["taps"], layout["kernels"])
    chip, core, view_here = position(cores)
    where = view_here * cores + core
    has_top = (chip > 0).astype(jnp.float32)
    has_bottom = (chip < layout["bricks"] // cores - 1).astype(jnp.float32)
    first = core == 0
    radius = taps // 2
    direct = decode_estimate(across[core])
    relayed = decode_estimate(passed[...])
    rows = (jnp.where(first, direct, relayed)[mine.shape[0] - radius :] * has_top,
            jnp.where(first, mine[...], partner[...]), jnp.where(first, partner[...], mine[...]),
            jnp.where(first, relayed, direct)[: 2 * radius] * has_bottom)
    for view in range(views):
        base = view * layout["table"]

        def one_plane(plane, carry):
            pick = table[base + layout["index_at"] + where * part + plane].astype(jnp.int32)
            for axis, target in enumerate((wx, wy)):
                begin = base + layout["bank_at"] + (axis * kernels + pick) * taps
                for tap in range(taps):
                    target[tap, pl.ds(view * part + plane, 1), :] = jnp.full(
                        (1, LANES), table[begin + tap], jnp.float32)
            return carry

        lax.fori_loop(0, part, one_plane, 0)
        planes = slice(view * part, (view + 1) * part)
        at = 0
        for piece in rows:
            field[at : at + piece.shape[0], planes, :] = piece
            at += piece.shape[0]
    rows_out, planes, columns = inverse.shape
    own_rows = cores * layout["rows_dev"]
    lane = lax.broadcasted_iota(jnp.int32, (SUBLANES, LANES), 1)
    place_blocks(layout, table, begins)

    def one_row(row, carry):
        wanted = jnp.where(row < own_rows, 1.0, has_bottom)
        for group in range(planes // SUBLANES):
            tiles = blur_row(field, row, group, wx, wy, taps, False, lane, columns // LANES)
            for col, value in enumerate(tiles):
                inverse[row, pl.ds(group * SUBLANES, SUBLANES), pl.ds(col * LANES, LANES)] = wanted / value
        return carry

    lax.fori_loop(0, rows_out, one_row, 0, unroll=2)


def ratio_row(layout, placed, inverse, field, turned, row):
    _, planes, columns = field.shape
    radius = layout["taps"] // 2
    block_width, pitch = layout["block_width"], layout["pitch"]
    per_tile = LANES // block_width
    groups = planes // per_tile
    lane = lax.broadcasted_iota(jnp.int32, (groups, LANES), 1)
    for col in range(columns // LANES):
        tiles = [
            placed[pl.ds((col * per_tile + k) * groups * pitch + row, groups, stride=pitch), :]
            for k in range(per_tile)
        ]
        step = per_tile // 2
        while step:
            width = step * block_width
            first_half = (lane // width) % 2 == 0
            mixed = list(tiles)
            for k in range(per_tile):
                if (k // step) % 2 == 0:
                    a, b = tiles[k], tiles[k + step]
                    mixed[k] = jnp.where(first_half, a, pltpu.roll(b, width, 1))
                    mixed[k + step] = jnp.where(first_half, pltpu.roll(a, LANES - width, 1), b)
            tiles = mixed
            step //= 2
        for k, value in enumerate(tiles):
            turned[pl.ds(col * planes + k, groups, stride=per_tile), :] = value
    for col in range(columns // LANES):
        for group in range(planes // SUBLANES):
            measured = turned[pl.ds(col * planes + group * SUBLANES, SUBLANES), :]
            planes_at = pl.ds(group * SUBLANES, SUBLANES)
            field[row + radius, planes_at, pl.ds(col * LANES, LANES)] = (
                measured * tile(inverse, row, group, col))


def ratio_body(layout, begins, arrived, inverse, cleared, placed, field, upward, downward, turned):
    views, cores, slots, taps = layout["views"], layout["cores"], layout["slots"], layout["taps"]
    bricks, rows_dev = layout["bricks"], layout["rows_dev"]
    radius = taps // 2
    per_tile = LANES // layout["block_width"]
    depth_tiles = layout["part"] // per_tile
    pitch = layout["pitch"]

    def one_source(source, carry):
        adds = []
        for view in range(views):
            for slot in range(slots):
                begin = begins[(source * views + view) * slots + slot]
                values = arrived[source * views + view, slot].astype(jnp.float32)
                for z_tile in range(depth_tiles):
                    adds.append((
                        begin + z_tile * pitch,
                        values[:, z_tile * LANES : (z_tile + 1) * LANES]))
        held = [placed[pl.ds(begin, rows_dev), :] for begin, _ in adds]
        for (begin, value), old in zip(adds, held):
            placed[pl.ds(begin, rows_dev), :] = old + value
        return carry

    lax.fori_loop(0, bricks, one_source, 0, unroll=UNROLL)
    own_rows = cores * rows_dev
    for target, begin in ((upward, own_rows - radius), (downward, 0)):

        def one_row(row, carry):
            ratio_row(layout, placed, inverse, field, turned, row + begin)
            target[row] = encode_ratio(field[row + begin + radius], bricks, taps)
            return carry

        lax.fori_loop(0, target.shape[0], one_row, 0, unroll=UNROLL)


def own_body(layout, placed, inverse, edges, wx, wy, field, done, turned):
    rows, planes, columns = done.shape
    radius = layout["taps"] // 2
    lane = lax.broadcasted_iota(jnp.int32, (SUBLANES, LANES), 1)
    field[0:radius] = jnp.zeros((radius, planes, columns), jnp.float32)

    def inner_row(row, carry):
        ratio_row(layout, placed, inverse, field, turned, row)
        return carry

    lax.fori_loop(radius, rows - radius, inner_row, 0)

    def one_row(row, carry):
        for group in range(planes // SUBLANES):
            tiles = blur_row(field, row, group, wx, wy, layout["taps"], True, lane, columns // LANES)
            for col, value in enumerate(tiles):
                done[row, pl.ds(group * SUBLANES, SUBLANES), pl.ds(col * LANES, LANES)] = value
        return carry

    lax.fori_loop(0, rows, one_row, 0, unroll=2)


def rest_body(layout, flip, done, before, after, wx, wy, source, target, reach, total):
    views, part, cores, taps = layout["views"], layout["part"], layout["cores"], layout["taps"]
    bricks, rows_dev = layout["bricks"], layout["rows_dev"]
    _, planes, columns = done.shape
    radius = taps // 2
    chip, core, _ = position(cores)
    lane = lax.broadcasted_iota(jnp.int32, (SUBLANES, LANES), 1)
    cols = columns // LANES

    def add_received(half):
        message, there = (
            (after, chip < bricks // cores - 1) if half else (before, chip > 0))
        mask = there.astype(jnp.float32)

        def one_message_row(row, carry):
            reach[row] = decode_ratio(message[row], bricks, taps) * mask
            return carry

        lax.fori_loop(0, message.shape[0], one_message_row, 0, unroll=UNROLL)
        first = rows_dev if half else -radius

        def one_group(group, carry):
            planes_at = pl.ds(pl.multiple_of(group * SUBLANES, SUBLANES), SUBLANES)
            for row in range(rows_dev):
                result = [
                    done[half * rows_dev + row, planes_at, pl.ds(col * LANES, LANES)]
                    for col in range(cols)
                ]
                sums = None
                for tap in range(taps):
                    at = row + radius - tap - first
                    if not 0 <= at < message.shape[0]:
                        continue
                    weight = wx[tap, planes_at, :]
                    terms = [
                        weight * reach[at, planes_at, pl.ds(col * LANES, LANES)] for col in range(cols)]
                    sums = terms if sums is None else [a + b for a, b in zip(sums, terms)]
                for tap in range(taps if sums else 0):
                    weight = wy[tap, planes_at, :]
                    moved = shifted(sums, lane, radius - tap)
                    result = [a + weight * m for a, m in zip(result, moved)]
                for col, value in enumerate(result):
                    total[row, planes_at, pl.ds(col * LANES, LANES)] = value
            return carry

        lax.fori_loop(0, planes // SUBLANES, one_group, 0)

    this = 1 - core if flip else core
    for half in range(cores):
        pl.when(this == half)(functools.partial(add_received, half))
    wide = lax.broadcasted_iota(jnp.int32, (part, LANES), 1)
    levels = jnp.zeros((part, LANES), jnp.float32)
    for row in range(rows_dev):
        value = source[row]
        for view in range(views):
            value = value * total[row, view * part : (view + 1) * part, :]
        target[:, row * columns : (row + 1) * columns], level = encode_rows(value)
        levels = jnp.where(wide == row, level, levels)
    target[:, rows_dev * columns :] = levels.astype(jnp.int32).astype(jnp.int16)


def join_body(places, *refs):
    _, core, view = position(2)
    count = len(places)
    sources, (out, held, sems) = refs[:count], refs[-3:]
    rows, columns = out.shape[0], out.shape[2]
    part = sources[0].shape[0]
    copies = []
    for index, (piece, (turn, flip)) in enumerate(zip(sources, places)):
        v = 1 - view if turn else view
        c = 1 - core if flip else core
        levels = piece[:, rows * columns :]
        for row in range(rows):
            held[index, row] = decode_row(piece[:, row * columns : (row + 1) * columns], levels, row)
        begin = pl.multiple_of((v * 2 + c) * part, part)
        copies.append(pltpu.make_async_copy(
            held.at[index], out.at[:, pl.ds(begin, part), :], sems.at[index]))
        copies[-1].start()
    for copy in copies:
        copy.wait()


def join(shape, part, places, pieces, out=None):
    rows, _, columns = shape
    count = len(pieces)
    return pl.pallas_call(
        functools.partial(join_body, places),
        out_shape=jax.ShapeDtypeStruct(shape, jnp.float32),
        in_specs=[VMEM] * count + ([] if out is None else [HBM]),
        out_specs=HBM,
        input_output_aliases={} if out is None else {count: 0},
        scratch_shapes=[
            pltpu.VMEM((count, rows, part, columns), jnp.float32), pltpu.SemaphoreType.DMA((count,))],
        compiler_params=GRANT,
        name="join",
    )(*near_core(*pieces), *([] if out is None else [out]))


def shards(estimate, camera_blocks, block_lists, block_offsets, psf_index, psf_bank):
    rows_dev, depth, columns = estimate.shape
    _, per_holder, block_rows, block_lanes = camera_blocks.shape
    bricks, slots = block_lists.shape[1], block_lists.shape[3]
    views = lax.axis_size("view")
    kernels, taps = psf_bank.shape[2:]
    radius = taps // 2
    cores = 2
    chips = bricks // cores
    part = depth // (cores * views)
    planes = views * part
    block_width = block_lanes // depth
    brick = lax.axis_index("brick")
    view = lax.axis_index("view")
    core = lax.rem(brick, cores)
    f32 = jnp.float32

    lists = block_lists[0].transpose(0, 2, 1)
    leaving = (chips, cores, views, slots, block_rows, part * block_width)
    outgoing = jax.ShapeDtypeStruct(leaving, camera_blocks.dtype)
    piece = pltpu.VMEM((rows_dev, part, columns), f32)
    coded = pltpu.VMEM((cores, rows_dev, part, columns), jnp.int16)
    packed, edges, mine, theirs = pl.pallas_call(
        pack_body,
        out_shape=[outgoing, coded, piece, piece],
        in_specs=[HBM] * 3,
        out_specs=[HBM] + [VMEM] * 3,
        scratch_shapes=[
            pltpu.VMEM(camera_blocks.shape[1:], camera_blocks.dtype),
            pltpu.VMEM(leaving, camera_blocks.dtype),
            pltpu.SMEM(lists.shape, jnp.int32),
            pltpu.SemaphoreType.DMA((5,)),
        ],
        compiler_params=GRANT,
        name="pack",
    )(*far_memory(lists, camera_blocks[0], estimate))
    swap = [(i, i ^ 1) for i in range(bricks)]
    packed = packed.reshape(bricks * views, slots, block_rows, part * block_width)
    across = lax.ppermute(edges, "brick", [
        (i, j) for i in range(bricks) for j in [i + 1 if i % cores else i - 1]
        if 0 <= j < bricks])
    partner = lax.ppermute(theirs, "brick", swap)
    arrived = lax.all_to_all(packed, ("brick", "view"), 0, 0, tiled=True)

    route = lax.dynamic_index_in_dim(lists, brick - core + cores - 1, 0, keepdims=False)
    pieces = [route.reshape(-1), block_offsets[0], psf_index[0], psf_bank[0].reshape(-1)]
    starts = [0]
    for piece in pieces:
        starts.append(starts[-1] + piece.shape[0])
    length = -(-starts[-1] // LANES) * LANES
    table = jnp.concatenate(
        [piece.astype(f32) for piece in pieces] + [jnp.zeros((length - starts[-1],), f32)])
    if views == 2:
        other = lax.ppermute(table, "view", [(0, 1), (1, 0)])
    layout = dict(
        views=views, part=part, cores=cores, taps=taps, kernels=kernels, slots=slots, bricks=bricks,
        per_holder=per_holder, rows_dev=rows_dev, block_width=block_width, table=length,
        offset_at=starts[1], index_at=starts[2], bank_at=starts[3],
        pitch=cores * rows_dev + radius + 1)

    up = [(i, i + cores) for i in range(bricks - cores)]
    down = [(i + cores, i) for i in range(bricks - cores)]
    passed = lax.ppermute(
        lax.dynamic_index_in_dim(across, 1 - core, 0, keepdims=False), "brick", swap)
    if views == 2:
        table = jnp.concatenate(
            [jnp.where(view == 0, table, other), jnp.where(view == 0, other, table)])
    else:
        table = lax.all_gather(table, "view", tiled=True)

    own_rows = cores * rows_dev
    rows_all = own_rows + radius
    groups = planes * block_width // LANES
    placing = pltpu.VMEM(((per_holder + 1) * groups * layout["pitch"], LANES), f32)
    inverse, wx, wy, begins = pl.pallas_call(
        functools.partial(blur_body, layout),
        out_shape=[
            pltpu.VMEM((rows_all, planes, columns), f32),
            pltpu.VMEM((taps, planes, LANES), f32),
            pltpu.VMEM((taps, planes, LANES), f32),
            pltpu.SMEM((bricks * views * slots,), jnp.int32),
        ],
        in_specs=[SMEM] + [VMEM] * 4,
        out_specs=[VMEM] * 3 + [SMEM],
        scratch_shapes=[pltpu.VMEM((rows_all + 2 * radius, planes, columns), f32)],
        compiler_params=GRANT,
        name="blur",
    )(table, *near_core(mine, partner, across, passed))

    edged = pltpu.VMEM((rows_all + radius, planes, columns), f32)
    turning = pltpu.VMEM((columns // LANES * planes, LANES), f32)
    cleared = pl.pallas_call(
        clear_body,
        out_shape=placing,
        in_specs=[VMEM],
        out_specs=VMEM,
        compiler_params=GRANT,
        name="clear",
    )(*near_core(wx))
    placed, field, upward, downward = pl.pallas_call(
        functools.partial(ratio_body, layout),
        out_shape=[
            placing,
            edged,
            pltpu.VMEM((2 * radius, planes, columns), jnp.int16),
            pltpu.VMEM((radius, planes, columns), jnp.int16),
        ],
        in_specs=[SMEM] + [VMEM] * 3,
        out_specs=[VMEM] * 4,
        input_output_aliases={3: 0},
        scratch_shapes=[turning],
        compiler_params=GRANT,
        name="ratio",
    )(pltpu.with_memory_space_constraint(begins, pltpu.SMEM), *near_core(arrived, inverse, cleared))

    before = lax.ppermute(upward, "brick", up)
    after = lax.ppermute(downward, "brick", down)
    _, done = pl.pallas_call(
        functools.partial(own_body, layout),
        out_shape=[edged, pltpu.VMEM((own_rows, planes, columns), f32)],
        in_specs=[VMEM] * 5,
        out_specs=[VMEM] * 2,
        input_output_aliases={2: 0},
        scratch_shapes=[turning],
        compiler_params=GRANT,
        name="own",
    )(*near_core(placed, inverse, field, wx, wy))

    def finished(flip, source):
        return pl.pallas_call(
            functools.partial(rest_body, layout, flip),
            out_shape=pltpu.VMEM((part, rows_dev * columns + LANES), jnp.int16),
            in_specs=[VMEM] * 6,
            out_specs=VMEM,
            scratch_shapes=[
                pltpu.VMEM((2 * radius, planes, columns), f32),
                pltpu.VMEM((rows_dev, planes, columns), f32),
            ],
            compiler_params=GRANT,
            name="rest",
        )(*near_core(done, before, after, wx, wy), source)

    if views == 2:
        turn = [(0, 1), (1, 0)]
        keep = finished(False, mine)
        far = lax.ppermute(keep, "view", turn)
        send = finished(True, partner)
        far_near = lax.ppermute(send, ("brick", "view"), [
            (i * views + j, (i ^ 1) * views + 1 - j)
            for i in range(bricks) for j in range(views)])
        near = lax.ppermute(send, "brick", swap)
        out = join(estimate.shape, part, ((False, False), (False, True)), (keep, near))
        out = join(estimate.shape, part, ((True, False),), (far,), out)
        return join(estimate.shape, part, ((True, True),), (far_near,), out)
    keep = finished(False, mine)
    near = lax.ppermute(finished(True, partner), "brick", swap)
    both = jnp.stack([jnp.where(core == 0, keep, near), jnp.where(core == 0, near, keep)])
    coded = lax.all_gather(both, "view").reshape((-1,) + keep.shape)
    rows = [
        jax.vmap(lambda piece, row=row: decode_row(
            piece[:, row * columns : (row + 1) * columns], piece[:, rows_dev * columns :], row))(coded)
        for row in range(rows_dev)
    ]
    return jnp.stack(rows).reshape(estimate.shape)


def solution(mesh):
    placed = (
        P("brick", None, None),
        P("view", "brick", None, None),
        P("view", None, None, None),
        P("view", None),
        P("view", None),
        P("view", None, None, None),
    )
    return jax.shard_map(
        shards, mesh=mesh, in_specs=placed, out_specs=P("brick", None, None), check_vma=False
    )
```
